32 devices in a mesh: fft: 16 (over z, x, core), grp: 2 (over y).
Axes of the slice: x: 2, y: 2, z: 4, core: 2. Of those that a mesh axis runs over, the one named last changes fastest.
Arguments:
- limbs_a: int32 [4096, 8192], P(('fft', 'grp')), may hold values from -128 to 127
- limbs_b: int32 [4096, 8192], P(('fft', 'grp')), may hold values from -128 to 127
Outputs:
- product: float32 [4096, 16384], P(('fft', 'grp'))
The draws below stay inside these ranges and needn't reach their ends.
All inputs are finite; a program needn't handle non-finite values.
Results may differ from the reference program's by a relative error of at most 0.000098.
Values sent between devices are 32-bit elements; how exact they have to be, the bound alone decides.
No kernel may reach another device: no remote copies, remote signals or barrier semaphores. Data moves between devices by JAX's collectives and lax.ppermute only.
A program may use at most 192 MiB of HBM per device.

```python
import jax
import jax.numpy as jnp
from jax import lax

ROWS = 16384
COLS = 4096


def set_ends(drawn, own_key, low, high):
    index_at = [jax.random.randint(jax.random.fold_in(own_key, axis), (), 0, length) for axis, length in enumerate(drawn.shape)]
    main_axis = drawn.shape.index(max(drawn.shape))
    neighbour = index_at[:main_axis] + [(index_at[main_axis] + 1) % drawn.shape[main_axis]] + index_at[main_axis + 1:]
    return drawn.at[tuple(index_at)].set(low).at[tuple(neighbour)].set(high)


def setup_inputs(seed: int = 0) -> dict:
    keys = jax.random.split(jax.random.key(seed), 3)
    return {
        "limbs_a": set_ends(jax.random.randint(keys[0], (COLS, ROWS // 2), -128, 128), jax.random.fold_in(keys[0], 1), -128, 127).astype(jnp.int32),
        "limbs_b": set_ends(jax.random.randint(keys[1], (COLS, ROWS // 2), -128, 128), jax.random.fold_in(keys[1], 1), -128, 127).astype(jnp.int32),
    }


def reference(limbs_a, limbs_b):
    padding = jnp.zeros(limbs_a.shape, jnp.float32)
    digits_a = jnp.concatenate([limbs_a.astype(jnp.float32), padding], axis=1).T.reshape(-1)
    digits_b = jnp.concatenate([limbs_b.astype(jnp.float32), padding], axis=1).T.reshape(-1)
    signal = lax.complex(digits_a, digits_b)
    spectrum = jnp.fft.fft(signal)
    mirror = jnp.conj(jnp.roll(jnp.flip(spectrum), 1))
    first_part = (spectrum + mirror) * 0.5
    second_part = (spectrum - mirror) * (-0.5j)
    pointwise = first_part * second_part
    total = ROWS * COLS
    coeffs = jnp.real(jnp.fft.ifft(pointwise)) * total
    out_scale = 1.0 / (total * 5461.25 * ((total // 2) ** 0.5))
    return (coeffs * out_scale).reshape(ROWS, COLS).T
```

```python
import functools
import math

import jax
import jax.numpy as jnp
import numpy as np
from jax import lax
from jax.experimental import pallas as pl
from jax.experimental.pallas import tpu as pltpu
from jax.sharding import PartitionSpec as P

DIGIT_VAR = 5461.25
INNER = 128
AXES = ("fft", "grp")
BF16 = jnp.bfloat16
F32 = jnp.float32


def split(value):
    high = value.astype(BF16)
    return (high, (value - high.astype(F32)).astype(BF16))


def three_dot(left, right, dims):
    def one(x, y):
        return lax.dot_general(x, y, (dims, ((), ())), preferred_element_type=F32)

    return one(left[0], right[0]) + (one(left[1], right[0]) + one(left[0], right[1]))


def rotate(re, im, turn):
    num, den = turn
    num = num % den
    if num == 0:
        return (re, im)
    if 4 * num == den:
        return (-im, re)
    if 2 * num == den:
        return (-re, -im)
    if 4 * num == 3 * den:
        return (im, -re)
    angle = 2.0 * math.pi * num / den
    cos, sin = (math.cos(angle), math.sin(angle))
    return (re * cos - im * sin, re * sin + im * cos)


def fft_list(values, sign):
    size = len(values)
    if size == 1:
        return values
    even = fft_list(values[0::2], sign)
    odd = fft_list(values[1::2], sign)
    low, high = ([], [])
    for k in range(size // 2):
        (er, ei), (r, i) = (even[k], odd[k])
        if 8 * k == size or 8 * k == 3 * size:
            root = math.sqrt(0.5)
            if 8 * k == size:
                tr, ti = ((r - sign * i) * root, (i + sign * r) * root)
            else:
                tr, ti = ((-r - sign * i) * root, (sign * r - i) * root)
            low.append((er + tr, ei + ti))
            high.append((er - tr, ei - ti))
        elif 4 * k == size:
            if sign > 0:
                low.append((er - i, ei + r))
                high.append((er + i, ei - r))
            else:
                low.append((er + i, ei - r))
                high.append((er - i, ei + r))
        else:
            tr, ti = rotate(r, i, (sign * k, size))
            low.append((er + tr, ei + ti))
            high.append((er - tr, ei - ti))
    return low + high


def times(x, y):
    return (x[0] * y[0] - x[1] * y[1], x[0] * y[1] + x[1] * y[0])


def times_conj(x, y):
    return (x[0] * y[0] + x[1] * y[1], x[1] * y[0] - x[0] * y[1])


def first_kernel(outer, a_ref, b_ref, cos_ref, sin_ref, sa_ref, sb_ref):
    for src, dst in ((a_ref, sa_ref), (b_ref, sb_ref)):
        terms = []
        for r in range(outer):
            digit = src[:, r * INNER : (r + 1) * INNER].astype(F32)
            angle = -2.0 * math.pi * r / (4 * outer)
            if r == 0:
                terms.append((digit, jnp.zeros_like(digit)))
            else:
                terms.append((digit * math.cos(angle), digit * math.sin(angle)))
        result = fft_list(terms, -1)
        for j in range(outer):
            re, im = times_conj(result[j], (cos_ref[j : j + 1, :], sin_ref[j : j + 1, :]))
            dst[j, :, :INNER] = re
            dst[j, :, INNER:] = im


def first_stage(limbs_a, limbs_b, cos, sin):
    cols, length = limbs_a.shape
    outer = length // INNER
    rows = 8
    in_spec = pl.BlockSpec((rows, length), lambda i: (i, 0))
    table = pl.BlockSpec((outer, INNER), lambda i: (0, 0))
    out_spec = pl.BlockSpec((outer, rows, 2 * INNER), lambda i: (0, i, 0))
    out = jax.ShapeDtypeStruct((outer, cols, 2 * INNER), F32)
    return pl.pallas_call(
        functools.partial(first_kernel, outer),
        grid=(cols // rows,),
        in_specs=[in_spec, in_spec, table, table],
        out_specs=[out_spec, out_spec],
        out_shape=[out, out],
        cost_estimate=pl.CostEstimate(
            flops=100 * cols * length, bytes_accessed=24 * cols * length, transcendentals=0
        ),
        name="first_stage",
    )(limbs_a, limbs_b, cos, sin)


def second_kernel(group, sa_ref, sb_ref, table_ref, out_ref, high_ref, low_ref):
    @pl.when(pl.program_id(0) == 0)
    def _():
        high_ref[...], low_ref[...] = split(table_ref[...])

    cols = sa_ref.shape[2]
    table = (high_ref[...], low_ref[...])
    for g in range(group):
        for at, src in ((0, sa_ref), (2, sb_ref)):
            result = three_dot(table, split(src[g, 0]), ((1,), (1,)))
            out_ref[g, at] = result[:INNER]
            out_ref[g, at + 1] = result[INNER:]


def second_stage(sa, sb, table, chunk, chunks):
    outer, cols, width = sa.shape
    count = outer // chunks
    group = 2 if count % 2 == 0 else 1
    shaped = (count, chunks, cols, width)
    spec = pl.BlockSpec((group, 1, cols, width), lambda i: (i, chunk, 0, 0))
    return pl.pallas_call(
        functools.partial(second_kernel, group),
        grid=(count // group,),
        in_specs=[spec, spec, pl.BlockSpec((width, width), lambda i: (0, 0))],
        out_specs=pl.BlockSpec((group, 4, INNER, cols), lambda i: (i, 0, 0, 0)),
        out_shape=jax.ShapeDtypeStruct((count, 4, INNER, cols), F32),
        scratch_shapes=[pltpu.VMEM((width, width), BF16)] * 2,
        cost_estimate=pl.CostEstimate(
            flops=12 * count * cols * width * width, bytes_accessed=16 * count * cols * width, transcendentals=0
        ),
        name="second_stage",
    )(sa.reshape(shaped), sb.reshape(shaped), table)


def middle_kernel(devices, x_ref, ka_cos, ka_sin, q_cos, q_sin, fh, fl, ih, il, v_ref, ya, yb):
    cols = x_ref.shape[3]
    rows = x_ref.shape[2]
    q_turn = (q_cos[...], q_sin[...])

    def turn_of(k):
        return times((ka_cos[k : k + 1, :], ka_sin[k : k + 1, :]), q_turn)

    for at, dst in ((0, ya), (2, yb)):
        result = fft_list([(x_ref[d, at], x_ref[d, at + 1]) for d in range(devices)], -1)
        for k in range(devices):
            re, im = times_conj(result[k], turn_of(k))
            dst[k * rows : (k + 1) * rows, :cols] = re
            dst[k * rows : (k + 1) * rows, cols:] = im
    forward = (fh[...], fl[...])
    inverse = (ih[...], il[...])
    a = three_dot(split(ya[...]), forward, ((1,), (0,)))
    b = three_dot(split(yb[...]), forward, ((1,), (0,)))
    re, im = times((a[:, :cols], a[:, cols:]), (b[:, :cols], b[:, cols:]))
    ya[:, :cols] = re
    ya[:, cols:] = im
    yb[...] = three_dot(split(ya[...]), inverse, ((1,), (0,)))
    terms = []
    for k in range(devices):
        part = slice(k * rows, (k + 1) * rows)
        terms.append(times((yb[part, :cols], yb[part, cols:]), turn_of(k)))
    result = fft_list(terms, 1)
    for d in range(devices):
        v_ref[d, 0] = result[d][0]
        v_ref[d, 1] = result[d][1]


def middle_stage(x, ka_cos, ka_sin, q_cos, q_sin, tables):
    devices, _, count, cols = x.shape
    rows = 8
    whole = lambda t: pl.BlockSpec(t.shape, lambda i: (0, 0))
    q_spec = pl.BlockSpec((rows, cols), lambda i: (i, 0))
    return pl.pallas_call(
        functools.partial(middle_kernel, devices),
        grid=(count // rows,),
        in_specs=[
            pl.BlockSpec((devices, 4, rows, cols), lambda i: (0, 0, i, 0)),
            whole(ka_cos),
            whole(ka_sin),
            q_spec,
            q_spec,
        ]
        + [whole(t) for t in tables],
        out_specs=pl.BlockSpec((devices, 2, rows, cols), lambda i: (0, 0, i, 0)),
        out_shape=jax.ShapeDtypeStruct((devices, 2, count, cols), F32),
        scratch_shapes=[pltpu.VMEM((devices * rows, 2 * cols), F32)] * 2,
        cost_estimate=pl.CostEstimate(
            flops=36 * devices * count * cols * cols * 4, bytes_accessed=24 * devices * count * cols, transcendentals=0
        ),
        name="middle_stage",
    )(x, ka_cos, ka_sin, q_cos, q_sin, *tables)


def third_kernel(group, v_ref, table_ref, cos_ref, sin_ref, g_ref, high_ref, low_ref):
    @pl.when(pl.program_id(0) == 0)
    def _():
        high_ref[...], low_ref[...] = split(table_ref[...])

    table = (high_ref[...], low_ref[...])
    for g in range(group):
        stacked = jnp.concatenate([v_ref[g, 0].T, v_ref[g, 1].T], axis=1)
        result = three_dot(split(stacked), table, ((1,), (0,)))
        turn = (cos_ref[g], sin_ref[g])
        re, im = times((result[:, :INNER], result[:, INNER:]), turn)
        g_ref[g, :, :INNER] = re
        g_ref[g, :, INNER:] = im


def third_stage(v, table, cos, sin, chunk, chunks):
    count, _, _, cols = v.shape
    group = 2 if count % 2 == 0 else 1
    width = 2 * INNER
    turns = pl.BlockSpec((group, 1, INNER), lambda i: (i, 0, 0))
    cos = cos.reshape(count, chunks, INNER)[:, chunk][:, None]
    sin = sin.reshape(count, chunks, INNER)[:, chunk][:, None]
    return pl.pallas_call(
        functools.partial(third_kernel, group),
        grid=(count // group,),
        in_specs=[
            pl.BlockSpec((group, 2, INNER, cols), lambda i: (i, 0, 0, 0)),
            pl.BlockSpec((width, width), lambda i: (0, 0)),
            turns,
            turns,
        ],
        out_specs=pl.BlockSpec((group, cols, width), lambda i: (i, 0, 0)),
        out_shape=jax.ShapeDtypeStruct((count, cols, width), F32),
        scratch_shapes=[pltpu.VMEM((width, width), BF16)] * 2,
        cost_estimate=pl.CostEstimate(
            flops=6 * count * cols * width * width, bytes_accessed=8 * count * cols * width, transcendentals=0
        ),
        name="third_stage",
    )(v, table, cos, sin)


def last_kernel(outer, scale, *refs):
    out_ref = refs[-1]
    chunks = len(refs) - 1
    terms = []
    for j in range(outer):
        src = refs[j % chunks]
        terms.append((src[j // chunks, :, :INNER], src[j // chunks, :, INNER:]))
    result = fft_list(terms, 1)
    for r in range(outer):
        angle = 2.0 * math.pi * r / (4 * outer)
        cos, sin = (math.cos(angle) * scale, math.sin(angle) * scale)
        re, im = result[r]
        at = r * INNER
        out_ref[:, at : at + INNER] = re * cos - im * sin
        at = at + outer * INNER
        out_ref[:, at : at + INNER] = -(re * sin + im * cos)


def last_stage(parts, scale):
    chunks = len(parts)
    count, cols, width = parts[0].shape
    outer = count * chunks
    rows = 8
    length = outer * INNER
    return pl.pallas_call(
        functools.partial(last_kernel, outer, scale),
        grid=(cols // rows,),
        in_specs=[pl.BlockSpec((count, rows, width), lambda i: (0, i, 0))] * chunks,
        out_specs=pl.BlockSpec((rows, 2 * length), lambda i: (i, 0)),
        out_shape=jax.ShapeDtypeStruct((cols, 2 * length), F32),
        cost_estimate=pl.CostEstimate(
            flops=100 * cols * length, bytes_accessed=16 * cols * length, transcendentals=0
        ),
        name="last_stage",
    )(*parts)


def turns(phase, modulus):
    angle = (phase % modulus).astype(F32) * (2.0 * math.pi / modulus)
    return (jnp.cos(angle), jnp.sin(angle))


def iota(shape, dim):
    return lax.broadcasted_iota(jnp.int32, shape, dim)


def row_turns(outer, devices, device):
    shape = (outer, INNER)
    phase = (4 * iota(shape, 0) + 1) * (devices * iota(shape, 1) + device)
    return turns(phase, 4 * outer * INNER * devices)


def row_table(devices, device):
    shape = (2 * INNER, 2 * INNER)
    row, col = (iota(shape, 0), iota(shape, 1))
    modulus = 4 * INNER * devices
    phase = 4 * (row % INNER) * (devices * (col % INNER) + device)
    quarter = INNER * devices * (row // INNER - col // INNER)
    angle = ((phase + quarter) % modulus).astype(F32) * (2.0 * math.pi / modulus)
    return jnp.cos(angle)


def spectral_turns(local, cols, devices, device, outer, total):
    shape = (local, cols)
    at = iota(shape, 0) + device * local
    freq = at // INNER + outer * (at % INNER)
    return turns(iota(shape, 1) * (4 * freq + 1), total)


def np_split(value):
    high = value.astype(np.float32).astype(BF16)
    low = (value - high.astype(np.float64)).astype(np.float32).astype(BF16)
    return (high, low)


def column_tables(cols, devices):
    k = np.arange(devices)[:, None] * np.arange(cols)[None, :]
    angle = 2.0 * np.pi * k / (cols * devices)
    n = np.arange(cols)
    theta = 2.0 * np.pi * (n[:, None] * n[None, :] % cols) / cols
    forward = np.block([[np.cos(theta), -np.sin(theta)], [np.sin(theta), np.cos(theta)]])
    tables = np_split(forward) + np_split(forward.T)
    return (np.cos(angle).astype(np.float32), np.sin(angle).astype(np.float32), tables)


def exchange(value):
    return lax.all_to_all(value, AXES, split_axis=0, concat_axis=0, tiled=True)


def on_device(limbs_a, limbs_b):
    devices = lax.axis_size(AXES)
    device = lax.axis_index(AXES)
    cols, length = limbs_a.shape
    outer = length // INNER
    total = length * cols * devices
    scale = 1.0 / (total * DIGIT_VAR * math.sqrt(total))
    chunks = max(1, outer // devices)
    pieces = max(1, devices // outer)
    local = length // devices
    cos, sin = row_turns(outer, devices, device)
    table = row_table(devices, device)
    ka_cos, ka_sin, tables = column_tables(cols, devices)
    q_cos, q_sin = spectral_turns(local, cols, devices, device, outer, 4 * total)
    each = local // chunks

    sa, sb = first_stage(limbs_a, limbs_b, cos, sin)
    arrived = []
    for h in range(chunks):
        x = second_stage(sa, sb, table, h, chunks)
        if pieces > 1:
            x = x.reshape(outer, 4, pieces, each, cols).transpose(0, 2, 1, 3, 4)
            x = x.reshape(devices, 4, each, cols)
        arrived.append(exchange(x))
    back = []
    for h in range(chunks):
        part = slice(h * each, (h + 1) * each)
        v = middle_stage(arrived[h], ka_cos, ka_sin, q_cos[part], q_sin[part], tables)
        back.append(exchange(v))
    parts = []
    for h in range(chunks):
        v = back[h]
        if pieces > 1:
            v = v.reshape(outer, pieces, 2, each, cols).transpose(0, 2, 1, 3, 4)
            v = v.reshape(outer, 2, INNER, cols)
        parts.append(third_stage(v, table, cos, sin, h, chunks))
    return last_stage(parts, scale)


def solution(mesh):
    placed = P(AXES, None)
    return jax.shard_map(
        on_device, mesh=mesh, in_specs=(placed, placed), out_specs=placed, check_vma=False
    )
```

```python
import functools
import math

import jax
import jax.numpy as jnp
import numpy as np
from jax import lax
from jax.experimental import pallas as pl
from jax.experimental.pallas import tpu as pltpu
from jax.sharding import PartitionSpec as P

DIGIT_VAR = 5461.25
INNER = 128
ROWS_STEP = 8
AXES = ("fft", "grp")
BF16 = jnp.bfloat16
F32 = jnp.float32


def split(value):
    high = value.astype(BF16)
    return (high, (value - high.astype(F32)).astype(BF16))


def three_dot(left, right, dims):
    def one(x, y):
        return lax.dot_general(x, y, (dims, ((), ())), preferred_element_type=F32)

    return one(left[0], right[0]) + (one(left[1], right[0]) + one(left[0], right[1]))


def rotate(re, im, turn):
    num, den = turn
    num = num % den
    if num == 0:
        return (re, im)
    if 4 * num == den:
        return (-im, re)
    if 2 * num == den:
        return (-re, -im)
    if 4 * num == 3 * den:
        return (im, -re)
    if 8 * num == den:
        return ((re - im) * math.sqrt(0.5), (re + im) * math.sqrt(0.5))
    angle = 2.0 * math.pi * num / den
    cos, sin = (math.cos(angle), math.sin(angle))
    return (re * cos - im * sin, re * sin + im * cos)


def fft_list(values, sign):
    size = len(values)
    if size == 1:
        return values
    even = fft_list(values[0::2], sign)
    odd = fft_list(values[1::2], sign)
    low, high = ([], [])
    for k in range(size // 2):
        (er, ei), (r, i) = (even[k], odd[k])
        if 8 * k == size or 8 * k == 3 * size:
            root = math.sqrt(0.5)
            if 8 * k == size:
                tr, ti = ((r - sign * i) * root, (i + sign * r) * root)
            else:
                tr, ti = ((-r - sign * i) * root, (sign * r - i) * root)
            low.append((er + tr, ei + ti))
            high.append((er - tr, ei - ti))
        elif 4 * k == size:
            if sign > 0:
                low.append((er - i, ei + r))
                high.append((er + i, ei - r))
            else:
                low.append((er + i, ei - r))
                high.append((er - i, ei + r))
        else:
            tr, ti = rotate(r, i, (sign * k, size))
            low.append((er + tr, ei + ti))
            high.append((er - tr, ei - ti))
    return low + high


def times(x, y):
    return (x[0] * y[0] - x[1] * y[1], x[0] * y[1] + x[1] * y[0])


def times_conj(x, y):
    return (x[0] * y[0] + x[1] * y[1], x[1] * y[0] - x[0] * y[1])


def head_kernel(outer, chunk, chunks, steps, a_ref, b_ref, cos_ref, sin_ref, table_ref, out_ref, rows_ref, high_ref, low_ref):
    step = pl.program_id(0)
    cols = rows_ref.shape[1] // 2
    count = outer // chunks
    group = out_ref.shape[0]

    @pl.when(step == 0)
    def _():
        high_ref[...], low_ref[...] = split(table_ref[...])

    @pl.when(step < steps)
    def _():
        for side, src in ((0, a_ref), (cols, b_ref)):
            terms = []
            for r in range(count):
                re = im = None
                for s in range(chunks):
                    at = (r + s * count) * INNER
                    digit = src[:, at : at + INNER].astype(F32)
                    if s == 0:
                        re = digit
                    else:
                        angle = -2.0 * math.pi * s * (4 * chunk + 1) / (4 * chunks)
                        re = re + digit * math.cos(angle)
                        new = digit * math.sin(angle)
                        im = new if im is None else im + new
                angle = -2.0 * math.pi * r * (4 * chunk + 1) / (4 * outer)
                cos, sin = (math.cos(angle), math.sin(angle))
                if im is None:
                    terms.append((re * cos, re * sin))
                elif r == 0:
                    terms.append((re, im))
                else:
                    terms.append((re * cos - im * sin, re * sin + im * cos))
            result = fft_list(terms, -1)
            at = pl.ds(pl.multiple_of(side + step * ROWS_STEP, ROWS_STEP), ROWS_STEP)
            for j in range(count):
                re, im = times_conj(result[j], (cos_ref[j : j + 1, :], sin_ref[j : j + 1, :]))
                rows_ref[j, at, :INNER] = re
                rows_ref[j, at, INNER:] = im

    @pl.when(step >= steps)
    def _():
        table = (high_ref[...], low_ref[...])
        for g in range(group):
            j = (step - steps) * group + g
            if cols % INNER == 0:
                both = three_dot(table, split(rows_ref[j]), ((1,), (1,)))
                sides = (both[:, :cols], both[:, cols:])
            else:
                sides = tuple(
                    three_dot(table, split(rows_ref[j, at : at + cols]), ((1,), (1,))) for at in (0, cols)
                )
            for at in (0, 1):
                out_ref[g, 2 * at] = sides[at][:INNER]
                out_ref[g, 2 * at + 1] = sides[at][INNER:]


def head_stage(limbs_a, limbs_b, cos, sin, table, chunk, chunks):
    cols, length = limbs_a.shape
    outer = length // INNER
    count = outer // chunks
    steps = cols // ROWS_STEP
    group = 2 if count % 2 == 0 else 1
    width = 2 * INNER
    in_spec = pl.BlockSpec((ROWS_STEP, length), lambda i: (jnp.minimum(i, steps - 1), 0))
    turns_spec = pl.BlockSpec((count, INNER), lambda i: (0, 0))
    return pl.pallas_call(
        functools.partial(head_kernel, outer, chunk, chunks, steps),
        grid=(steps + count // group,),
        in_specs=[in_spec, in_spec, turns_spec, turns_spec, pl.BlockSpec((width, width), lambda i: (0, 0))],
        out_specs=pl.BlockSpec((group, 4, INNER, cols), lambda i: (jnp.maximum(i - steps, 0), 0, 0, 0)),
        out_shape=jax.ShapeDtypeStruct((count, 4, INNER, cols), F32),
        scratch_shapes=[pltpu.VMEM((count, 2 * cols, width), F32)] + [pltpu.VMEM((width, width), BF16)] * 2,
        cost_estimate=pl.CostEstimate(
            flops=12 * count * cols * width * width, bytes_accessed=16 * count * cols * width, transcendentals=0
        ),
        name="head_stage",
    )(limbs_a, limbs_b, cos, sin, table)


def middle_kernel(devices, x_ref, ka_cos, ka_sin, q_cos, q_sin, fh, fl, ih, il, v_ref, ya, yb):
    cols = x_ref.shape[3]
    rows = x_ref.shape[2]
    q_turn = (q_cos[...], q_sin[...])

    def turn_of(k):
        return times((ka_cos[k : k + 1, :], ka_sin[k : k + 1, :]), q_turn)

    for at, dst in ((0, ya), (2, yb)):
        result = fft_list([(x_ref[d, at], x_ref[d, at + 1]) for d in range(devices)], -1)
        for k in range(devices):
            re, im = times_conj(result[k], turn_of(k))
            dst[k * rows : (k + 1) * rows, :cols] = re
            dst[k * rows : (k + 1) * rows, cols:] = im
    forward = (fh[...], fl[...])
    inverse = (ih[...], il[...])
    a = three_dot(split(ya[...]), forward, ((1,), (0,)))
    b = three_dot(split(yb[...]), forward, ((1,), (0,)))
    re, im = times((a[:, :cols], a[:, cols:]), (b[:, :cols], b[:, cols:]))
    ya[:, :cols] = re
    ya[:, cols:] = im
    yb[...] = three_dot(split(ya[...]), inverse, ((1,), (0,)))
    terms = []
    for k in range(devices):
        part = slice(k * rows, (k + 1) * rows)
        terms.append(times((yb[part, :cols], yb[part, cols:]), turn_of(k)))
    result = fft_list(terms, 1)
    for d in range(devices):
        v_ref[d, 0] = result[d][0]
        v_ref[d, 1] = result[d][1]


def middle_stage(x, ka_cos, ka_sin, q_cos, q_sin, tables):
    devices, _, count, cols = x.shape
    rows = 8
    whole = lambda t: pl.BlockSpec(t.shape, lambda i: (0, 0))
    q_spec = pl.BlockSpec((rows, cols), lambda i: (i, 0))
    return pl.pallas_call(
        functools.partial(middle_kernel, devices),
        grid=(count // rows,),
        in_specs=[
            pl.BlockSpec((devices, 4, rows, cols), lambda i: (0, 0, i, 0)),
            whole(ka_cos),
            whole(ka_sin),
            q_spec,
            q_spec,
        ]
        + [whole(t) for t in tables],
        out_specs=pl.BlockSpec((devices, 2, rows, cols), lambda i: (0, 0, i, 0)),
        out_shape=jax.ShapeDtypeStruct((devices, 2, count, cols), F32),
        scratch_shapes=[pltpu.VMEM((devices * rows, 2 * cols), F32)] * 2,
        cost_estimate=pl.CostEstimate(
            flops=36 * devices * count * cols * cols * 4, bytes_accessed=24 * devices * count * cols, transcendentals=0
        ),
        name="middle_stage",
    )(x, ka_cos, ka_sin, q_cos, q_sin, *tables)


def tail_kernel(outer, chunk, steps, v_ref, table_ref, cos_ref, sin_ref, *refs):
    *others, out_ref, rows_ref, high_ref, low_ref = refs
    chunks = len(others) + 1
    step = pl.program_id(0)
    count, cols, _ = rows_ref.shape
    group = v_ref.shape[0]

    @pl.when(step == 0)
    def _():
        high_ref[...], low_ref[...] = split(table_ref[...])

    @pl.when(step < steps)
    def _():
        table = (high_ref[...], low_ref[...])
        stacked = jnp.concatenate(
            [jnp.concatenate([v_ref[g, 0].T, v_ref[g, 1].T], axis=1) for g in range(group)], axis=0
        )
        result = three_dot(split(stacked), table, ((1,), (0,)))
        for g in range(group):
            j = step * group + g
            part = result[g * cols : (g + 1) * cols]
            turn = (cos_ref[pl.ds(j, 1), :], sin_ref[pl.ds(j, 1), :])
            re, im = times((part[:, :INNER], part[:, INNER:]), turn)
            rows_ref[j, :, :INNER] = re
            rows_ref[j, :, INNER:] = im

    @pl.when(step >= steps)
    def _():
        at = pl.ds(pl.multiple_of((step - steps) * ROWS_STEP, ROWS_STEP), ROWS_STEP)
        result = fft_list([(rows_ref[j, at, :INNER], rows_ref[j, at, INNER:]) for j in range(count)], 1)
        for r in range(count):
            mine = rotate(*result[r], (r * (4 * chunk + 1), 4 * outer))
            if out_ref.ndim == 3:
                out_ref[r, :, :INNER] = mine[0]
                out_ref[r, :, INNER:] = mine[1]
                continue
            sums = fft_list([(o[r, :, :INNER], o[r, :, INNER:]) for o in others] + [mine], 1)
            for s in range(chunks):
                re, im = rotate(*sums[s], (s, 4 * chunks))
                low = (r + s * count) * INNER
                high = low + outer * INNER
                out_ref[:, low : low + INNER] = re
                out_ref[:, high : high + INNER] = -im


def tail_stage(v, table, cos, sin, others, chunk, chunks):
    count, _, _, cols = v.shape
    outer = count * chunks
    group = 4 if count % 4 == 0 else 1
    width = 2 * INNER
    steps = count // group
    final = chunk == chunks - 1
    later = lambda i: jnp.maximum(i - steps, 0)
    turns_spec = pl.BlockSpec((count, INNER), lambda i: (0, 0))
    row_spec = pl.BlockSpec((count, ROWS_STEP, width), lambda i: (0, later(i), 0))
    if final:
        out_spec = pl.BlockSpec((ROWS_STEP, outer * width), lambda i: (later(i), 0))
        out_shape = jax.ShapeDtypeStruct((cols, outer * width), F32)
    else:
        out_spec = row_spec
        out_shape = jax.ShapeDtypeStruct((count, cols, width), F32)
    others = others if final else []
    return pl.pallas_call(
        functools.partial(tail_kernel, outer, chunk, steps),
        grid=(steps + cols // ROWS_STEP,),
        in_specs=[
            pl.BlockSpec((group, 2, INNER, cols), lambda i: (jnp.minimum(i, steps - 1), 0, 0, 0)),
            pl.BlockSpec((width, width), lambda i: (0, 0)),
            turns_spec,
            turns_spec,
        ]
        + [row_spec] * len(others),
        out_specs=out_spec,
        out_shape=out_shape,
        scratch_shapes=[pltpu.VMEM((count, cols, width), F32)] + [pltpu.VMEM((width, width), BF16)] * 2,
        cost_estimate=pl.CostEstimate(
            flops=6 * count * cols * width * width, bytes_accessed=16 * count * cols * width, transcendentals=0
        ),
        name="tail_stage",
    )(v, table, cos, sin, *others)


def turns(phase, modulus):
    angle = (phase % modulus).astype(F32) * (2.0 * math.pi / modulus)
    return (jnp.cos(angle), jnp.sin(angle))


def iota(shape, dim):
    return lax.broadcasted_iota(jnp.int32, shape, dim)


def row_turns(outer, devices, device, chunk, chunks):
    shape = (outer // chunks, INNER)
    freq = chunks * iota(shape, 0) + chunk
    phase = (4 * freq + 1) * (devices * iota(shape, 1) + device)
    return turns(phase, 4 * outer * INNER * devices)


def row_table(devices, device):
    shape = (2 * INNER, 2 * INNER)
    row, col = (iota(shape, 0), iota(shape, 1))
    modulus = 4 * INNER * devices
    phase = 4 * (row % INNER) * (devices * (col % INNER) + device)
    quarter = INNER * devices * (row // INNER - col // INNER)
    angle = ((phase + quarter) % modulus).astype(F32) * (2.0 * math.pi / modulus)
    return jnp.cos(angle)


def spectral_turns(local, cols, devices, device, outer, total):
    shape = (local, cols)
    at = iota(shape, 0) + device * local
    freq = at // INNER + outer * (at % INNER)
    return turns(iota(shape, 1) * (4 * freq + 1), total)


def np_split(value):
    high = value.astype(np.float32).astype(BF16)
    low = (value - high.astype(np.float64)).astype(np.float32).astype(BF16)
    return (high, low)


def column_tables(cols, devices, scale):
    k = np.arange(devices)[:, None] * np.arange(cols)[None, :]
    angle = 2.0 * np.pi * k / (cols * devices)
    n = np.arange(cols)
    theta = 2.0 * np.pi * (n[:, None] * n[None, :] % cols) / cols
    forward = np.block([[np.cos(theta), -np.sin(theta)], [np.sin(theta), np.cos(theta)]])
    tables = np_split(forward) + np_split(forward.T * scale)
    return (np.cos(angle).astype(np.float32), np.sin(angle).astype(np.float32), tables)


def exchange(value):
    return lax.all_to_all(value, AXES, split_axis=0, concat_axis=0, tiled=True)


def on_device(limbs_a, limbs_b):
    devices = lax.axis_size(AXES)
    device = lax.axis_index(AXES)
    cols, length = limbs_a.shape
    outer = length // INNER
    total = length * cols * devices
    scale = 1.0 / (total * DIGIT_VAR * math.sqrt(total))
    chunks = max(1, outer // devices)
    pieces = max(1, devices // outer)
    local = length // devices
    rows = [row_turns(outer, devices, device, h, chunks) for h in range(chunks)]
    table = row_table(devices, device)
    ka_cos, ka_sin, tables = column_tables(cols, devices, scale)
    q_cos, q_sin = spectral_turns(local, cols, devices, device, outer, 4 * total)
    each = local // chunks

    arrived = []
    for h in range(chunks):
        x = head_stage(limbs_a, limbs_b, *rows[h], table, h, chunks)
        if pieces > 1:
            x = x.reshape(outer, 4, pieces, each, cols).transpose(0, 2, 1, 3, 4)
            x = x.reshape(devices, 4, each, cols)
        arrived.append(exchange(x))
    back = []
    for h in range(chunks):
        part = slice(h * each, (h + 1) * each)
        v = middle_stage(arrived[h], ka_cos, ka_sin, q_cos[part], q_sin[part], tables)
        back.append(exchange(v))
    parts = []
    for h in range(chunks):
        v = back[h]
        if pieces > 1:
            v = v.reshape(outer, pieces, 2, each, cols).transpose(0, 2, 1, 3, 4)
            v = v.reshape(outer, 2, INNER, cols)
        parts.append(tail_stage(v, table, *rows[h], parts, h, chunks))
    return parts[-1]


def solution(mesh):
    placed = P(AXES, None)
    return jax.shard_map(
        on_device, mesh=mesh, in_specs=(placed, placed), out_specs=placed, check_vma=False
    )
```

```python
import functools
import math

import jax
import jax.numpy as jnp
import numpy as np
from jax import lax
from jax.experimental import pallas as pl
from jax.experimental.pallas import tpu as pltpu
from jax.sharding import PartitionSpec as P

DIGIT_VAR = 5461.25
INNER = 128
SUBLANES = 8
HEAD_ROWS = 32
HEAD_GROUP = 4
TAIL_ROWS = 64
TAIL_GROUP = 16
AXES = ("fft", "grp")
BF16 = jnp.bfloat16
F32 = jnp.float32


def split(value):
    high = value.astype(BF16)
    return (high, (value - high.astype(F32)).astype(BF16))


def three_dot(left, right, dims):
    def one(x, y):
        return lax.dot_general(x, y, (dims, ((), ())), preferred_element_type=F32)

    return one(left[0], right[0]) + (one(left[1], right[0]) + one(left[0], right[1]))


def rotate(re, im, turn):
    num, den = turn
    num = num % den
    if num == 0:
        return (re, im)
    if 4 * num == den:
        return (-im, re)
    if 2 * num == den:
        return (-re, -im)
    if 4 * num == 3 * den:
        return (im, -re)
    if 8 * num == den:
        return ((re - im) * math.sqrt(0.5), (re + im) * math.sqrt(0.5))
    angle = 2.0 * math.pi * num / den
    cos, sin = (math.cos(angle), math.sin(angle))
    return (re * cos - im * sin, re * sin + im * cos)


def fft_list(values, sign):
    size = len(values)
    if size == 1:
        return values
    even = fft_list(values[0::2], sign)
    odd = fft_list(values[1::2], sign)
    low, high = ([], [])
    for k in range(size // 2):
        (er, ei), (r, i) = (even[k], odd[k])
        if 8 * k == size or 8 * k == 3 * size:
            root = math.sqrt(0.5)
            if 8 * k == size:
                tr, ti = ((r - sign * i) * root, (i + sign * r) * root)
            else:
                tr, ti = ((-r - sign * i) * root, (sign * r - i) * root)
            low.append((er + tr, ei + ti))
            high.append((er - tr, ei - ti))
        elif 4 * k == size:
            if sign > 0:
                low.append((er - i, ei + r))
                high.append((er + i, ei - r))
            else:
                low.append((er + i, ei - r))
                high.append((er - i, ei + r))
        else:
            tr, ti = rotate(r, i, (sign * k, size))
            low.append((er + tr, ei + ti))
            high.append((er - tr, ei - ti))
    return low + high


def times(x, y):
    return (x[0] * y[0] - x[1] * y[1], x[0] * y[1] + x[1] * y[0])


def times_conj(x, y):
    return (x[0] * y[0] + x[1] * y[1], x[1] * y[0] - x[0] * y[1])


def head_terms(src, own, outer, chunk, chunks):
    count = outer // chunks
    terms = []
    for r in range(count):
        re = im = None
        for s in range(chunks):
            at = (r + s * count) * INNER
            digit = src[own, at : at + INNER].astype(F32)
            if s == 0:
                re = digit
            else:
                angle = -2.0 * math.pi * s * (4 * chunk + 1) / (4 * chunks)
                re = re + digit * math.cos(angle)
                new = digit * math.sin(angle)
                im = new if im is None else im + new
        angle = -2.0 * math.pi * r * (4 * chunk + 1) / (4 * outer)
        cos, sin = (math.cos(angle), math.sin(angle))
        if im is None:
            terms.append((re * cos, re * sin))
        elif r == 0:
            terms.append((re, im))
        else:
            terms.append((re * cos - im * sin, re * sin + im * cos))
    return terms


def head_kernel(outer, chunk, chunks, steps, a_ref, b_ref, cos_ref, sin_ref, table_ref, out_ref, rows_ref, high_ref, low_ref):
    step = pl.program_id(0)
    cols = rows_ref.shape[1] // 2
    count = outer // chunks
    group = out_ref.shape[0]

    @pl.when(step == 0)
    def _():
        high_ref[...], low_ref[...] = split(table_ref[...])

    @pl.when(step < steps)
    def _():
        tile_rows = a_ref.shape[0]

        @pl.loop(0, tile_rows // SUBLANES)
        def _(i):
            own = pl.ds(pl.multiple_of(i * SUBLANES, SUBLANES), SUBLANES)
            for side, src in ((0, a_ref), (cols, b_ref)):
                terms = head_terms(src, own, outer, chunk, chunks)
                result = fft_list(terms, -1)
                at = pl.ds(pl.multiple_of(side + step * tile_rows + i * SUBLANES, SUBLANES), SUBLANES)
                for j in range(count):
                    re, im = times_conj(result[j], (cos_ref[j : j + 1, :], sin_ref[j : j + 1, :]))
                    rows_ref[j, at, :INNER] = re
                    rows_ref[j, at, INNER:] = im

    @pl.when(step >= steps)
    def _():
        table = (high_ref[...], low_ref[...])
        @pl.loop(0, group)
        def _(g):
            j = (step - steps) * group + g
            if cols % INNER == 0:
                both = three_dot(table, split(rows_ref[j]), ((1,), (1,)))
                sides = (both[:, :cols], both[:, cols:])
            else:
                sides = tuple(
                    three_dot(table, split(rows_ref[j, at : at + cols]), ((1,), (1,))) for at in (0, cols)
                )
            for at in (0, 1):
                out_ref[g, 2 * at] = sides[at][:INNER]
                out_ref[g, 2 * at + 1] = sides[at][INNER:]


def head_stage(limbs_a, limbs_b, cos, sin, table, chunk, chunks):
    cols, length = limbs_a.shape
    outer = length // INNER
    count = outer // chunks
    tile_rows = min(cols, HEAD_ROWS)
    steps = cols // tile_rows
    group = math.gcd(count, HEAD_GROUP)
    width = 2 * INNER
    in_spec = pl.BlockSpec((tile_rows, length), lambda i: (jnp.minimum(i, steps - 1), 0))
    turns_spec = pl.BlockSpec((count, INNER), lambda i: (0, 0))
    return pl.pallas_call(
        functools.partial(head_kernel, outer, chunk, chunks, steps),
        grid=(steps + count // group,),
        in_specs=[in_spec, in_spec, turns_spec, turns_spec, pl.BlockSpec((width, width), lambda i: (0, 0))],
        out_specs=pl.BlockSpec((group, 4, INNER, cols), lambda i: (jnp.maximum(i - steps, 0), 0, 0, 0)),
        out_shape=jax.ShapeDtypeStruct((count, 4, INNER, cols), F32),
        scratch_shapes=[pltpu.VMEM((count, 2 * cols, width), F32)] + [pltpu.VMEM((width, width), BF16)] * 2,
        cost_estimate=pl.CostEstimate(
            flops=12 * count * cols * width * width, bytes_accessed=16 * count * cols * width, transcendentals=0
        ),
        name="head_stage",
    )(limbs_a, limbs_b, cos, sin, table)


def middle_kernel(devices, x_ref, ka_cos, ka_sin, q_cos, q_sin, fh, fl, ih, il, v_ref, ya, yb):
    cols = x_ref.shape[3]
    rows = x_ref.shape[2]
    q_turn = (q_cos[...], q_sin[...])

    def turn_of(k):
        return times((ka_cos[k : k + 1, :], ka_sin[k : k + 1, :]), q_turn)

    for at, dst in ((0, ya), (2, yb)):
        result = fft_list([(x_ref[d, at], x_ref[d, at + 1]) for d in range(devices)], -1)
        for k in range(devices):
            re, im = times_conj(result[k], turn_of(k))
            dst[k * rows : (k + 1) * rows, :cols] = re
            dst[k * rows : (k + 1) * rows, cols:] = im
    forward = (fh[...], fl[...])
    inverse = (ih[...], il[...])
    a = three_dot(split(ya[...]), forward, ((1,), (0,)))
    b = three_dot(split(yb[...]), forward, ((1,), (0,)))
    re, im = times((a[:, :cols], a[:, cols:]), (b[:, :cols], b[:, cols:]))
    ya[:, :cols] = re
    ya[:, cols:] = im
    yb[...] = three_dot(split(ya[...]), inverse, ((1,), (0,)))
    terms = []
    for k in range(devices):
        part = slice(k * rows, (k + 1) * rows)
        terms.append(times((yb[part, :cols], yb[part, cols:]), turn_of(k)))
    result = fft_list(terms, 1)
    for d in range(devices):
        v_ref[d, 0] = result[d][0]
        v_ref[d, 1] = result[d][1]


def middle_stage(x, ka_cos, ka_sin, q_cos, q_sin, tables):
    devices, _, count, cols = x.shape
    rows = 8
    whole = lambda t: pl.BlockSpec(t.shape, lambda i: (0, 0))
    q_spec = pl.BlockSpec((rows, cols), lambda i: (i, 0))
    return pl.pallas_call(
        functools.partial(middle_kernel, devices),
        grid=(count // rows,),
        in_specs=[
            pl.BlockSpec((devices, 4, rows, cols), lambda i: (0, 0, i, 0)),
            whole(ka_cos),
            whole(ka_sin),
            q_spec,
            q_spec,
        ]
        + [whole(t) for t in tables],
        out_specs=pl.BlockSpec((devices, 2, rows, cols), lambda i: (0, 0, i, 0)),
        out_shape=jax.ShapeDtypeStruct((devices, 2, count, cols), F32),
        scratch_shapes=[pltpu.VMEM((devices * rows, 2 * cols), F32)] * 2,
        cost_estimate=pl.CostEstimate(
            flops=36 * devices * count * cols * cols * 4, bytes_accessed=24 * devices * count * cols, transcendentals=0
        ),
        name="middle_stage",
    )(x, ka_cos, ka_sin, q_cos, q_sin, *tables)


def tail_kernel(outer, chunk, steps, v_ref, table_ref, cos_ref, sin_ref, *refs):
    *others, out_ref, rows_ref, high_ref, low_ref = refs
    chunks = len(others) + 1
    step = pl.program_id(0)
    count, cols, _ = rows_ref.shape
    group = min(v_ref.shape[0], 4)

    @pl.when(step == 0)
    def _():
        high_ref[...], low_ref[...] = split(table_ref[...])

    @pl.when(step < steps)
    def _():
        table = (high_ref[...], low_ref[...])
        @pl.loop(0, v_ref.shape[0] // group)
        def _(i):
            stacked = jnp.concatenate(
                [
                    jnp.concatenate([v_ref[i * group + g, p].T for p in (0, 1)], axis=1)
                    for g in range(group)
                ],
                axis=0,
            )
            result = three_dot(split(stacked), table, ((1,), (0,)))
            for g in range(group):
                j = step * v_ref.shape[0] + i * group + g
                part = result[g * cols : (g + 1) * cols]
                turn = (cos_ref[pl.ds(j, 1), :], sin_ref[pl.ds(j, 1), :])
                re, im = times((part[:, :INNER], part[:, INNER:]), turn)
                rows_ref[j, :, :INNER] = re
                rows_ref[j, :, INNER:] = im

    @pl.when(step >= steps)
    def _():
        tile_rows = out_ref.shape[-2]

        @pl.loop(0, tile_rows // SUBLANES)
        def _(i):
            own = pl.ds(pl.multiple_of(i * SUBLANES, SUBLANES), SUBLANES)
            at = pl.ds(pl.multiple_of((step - steps) * tile_rows + i * SUBLANES, SUBLANES), SUBLANES)
            result = fft_list([(rows_ref[j, at, :INNER], rows_ref[j, at, INNER:]) for j in range(count)], 1)
            for r in range(count):
                mine = rotate(*result[r], (r * (4 * chunk + 1), 4 * outer))
                if out_ref.ndim == 3:
                    out_ref[r, own, :INNER] = mine[0]
                    out_ref[r, own, INNER:] = mine[1]
                    continue
                sums = fft_list([(o[r, own, :INNER], o[r, own, INNER:]) for o in others] + [mine], 1)
                for s in range(chunks):
                    re, im = rotate(*sums[s], (s, 4 * chunks))
                    low = (r + s * count) * INNER
                    high = low + outer * INNER
                    out_ref[own, low : low + INNER] = re
                    out_ref[own, high : high + INNER] = -im


def tail_stage(v, table, cos, sin, others, chunk, chunks):
    count, _, _, cols = v.shape
    outer = count * chunks
    group = math.gcd(count, TAIL_GROUP)
    tile_rows = min(cols, TAIL_ROWS)
    width = 2 * INNER
    steps = count // group
    final = chunk == chunks - 1
    later = lambda i: jnp.maximum(i - steps, 0)
    turns_spec = pl.BlockSpec((count, INNER), lambda i: (0, 0))
    row_spec = pl.BlockSpec((count, tile_rows, width), lambda i: (0, later(i), 0))
    if final:
        out_spec = pl.BlockSpec((tile_rows, outer * width), lambda i: (later(i), 0))
        out_shape = jax.ShapeDtypeStruct((cols, outer * width), F32)
    else:
        out_spec = row_spec
        out_shape = jax.ShapeDtypeStruct((count, cols, width), F32)
    others = others if final else []
    return pl.pallas_call(
        functools.partial(tail_kernel, outer, chunk, steps),
        grid=(steps + cols // tile_rows,),
        in_specs=[
            pl.BlockSpec((group, 2, INNER, cols), lambda i: (jnp.minimum(i, steps - 1), 0, 0, 0)),
            pl.BlockSpec((width, width), lambda i: (0, 0)),
            turns_spec,
            turns_spec,
        ]
        + [row_spec] * len(others),
        out_specs=out_spec,
        out_shape=out_shape,
        scratch_shapes=[pltpu.VMEM((count, cols, width), F32)] + [pltpu.VMEM((width, width), BF16)] * 2,
        cost_estimate=pl.CostEstimate(
            flops=6 * count * cols * width * width, bytes_accessed=16 * count * cols * width, transcendentals=0
        ),
        name="tail_stage",
    )(v, table, cos, sin, *others)


def turns(phase, modulus):
    angle = (phase % modulus).astype(F32) * (2.0 * math.pi / modulus)
    return (jnp.cos(angle), jnp.sin(angle))


def iota(shape, dim):
    return lax.broadcasted_iota(jnp.int32, shape, dim)


def row_turns(outer, devices, device, chunk, chunks):
    shape = (outer // chunks, INNER)
    freq = chunks * iota(shape, 0) + chunk
    phase = (4 * freq + 1) * (devices * iota(shape, 1) + device)
    return turns(phase, 4 * outer * INNER * devices)


def row_table(devices, device):
    shape = (2 * INNER, 2 * INNER)
    row, col = (iota(shape, 0), iota(shape, 1))
    modulus = 4 * INNER * devices
    phase = 4 * (row % INNER) * (devices * (col % INNER) + device)
    quarter = INNER * devices * (row // INNER - col // INNER)
    angle = ((phase + quarter) % modulus).astype(F32) * (2.0 * math.pi / modulus)
    return jnp.cos(angle)


def spectral_turns(local, cols, devices, device, outer, total):
    shape = (local, cols)
    at = iota(shape, 0) + device * local
    freq = at // INNER + outer * (at % INNER)
    return turns(iota(shape, 1) * (4 * freq + 1), total)


def np_split(value):
    high = value.astype(np.float32).astype(BF16)
    low = (value - high.astype(np.float64)).astype(np.float32).astype(BF16)
    return (high, low)


def column_tables(cols, devices, scale):
    k = np.arange(devices)[:, None] * np.arange(cols)[None, :]
    angle = 2.0 * np.pi * k / (cols * devices)
    n = np.arange(cols)
    theta = 2.0 * np.pi * (n[:, None] * n[None, :] % cols) / cols
    forward = np.block([[np.cos(theta), -np.sin(theta)], [np.sin(theta), np.cos(theta)]])
    tables = np_split(forward) + np_split(forward.T * scale)
    return (np.cos(angle).astype(np.float32), np.sin(angle).astype(np.float32), tables)


def exchange(value):
    return lax.all_to_all(value, AXES, split_axis=0, concat_axis=0, tiled=True)


def on_device(limbs_a, limbs_b):
    devices = lax.axis_size(AXES)
    device = lax.axis_index(AXES)
    cols, length = limbs_a.shape
    outer = length // INNER
    total = length * cols * devices
    scale = 1.0 / (total * DIGIT_VAR * math.sqrt(total))
    chunks = max(1, outer // devices)
    pieces = max(1, devices // outer)
    local = length // devices
    rows = [row_turns(outer, devices, device, h, chunks) for h in range(chunks)]
    table = row_table(devices, device)
    ka_cos, ka_sin, tables = column_tables(cols, devices, scale)
    q_cos, q_sin = spectral_turns(local, cols, devices, device, outer, 4 * total)
    each = local // chunks

    arrived = []
    for h in range(chunks):
        x = head_stage(limbs_a, limbs_b, *rows[h], table, h, chunks)
        if pieces > 1:
            x = x.reshape(outer, 4, pieces, each, cols).transpose(0, 2, 1, 3, 4)
            x = x.reshape(devices, 4, each, cols)
        arrived.append(exchange(x))
    back = []
    for h in range(chunks):
        part = slice(h * each, (h + 1) * each)
        v = middle_stage(arrived[h], ka_cos, ka_sin, q_cos[part], q_sin[part], tables)
        back.append(exchange(v))
    parts = []
    for h in range(chunks):
        v = back[h]
        if pieces > 1:
            v = v.reshape(outer, pieces, 2, each, cols).transpose(0, 2, 1, 3, 4)
            v = v.reshape(outer, 2, INNER, cols)
        parts.append(tail_stage(v, table, *rows[h], parts, h, chunks))
    return parts[-1]


def solution(mesh):
    placed = P(AXES, None)
    return jax.shard_map(
        on_device, mesh=mesh, in_specs=(placed, placed), out_specs=placed, check_vma=False
    )
```

```python
import functools
import math

import jax
import jax.numpy as jnp
import numpy as np
from jax import lax
from jax.experimental import pallas as pl
from jax.experimental.pallas import tpu as pltpu
from jax.sharding import PartitionSpec as P

DIGIT_VAR = 5461.25
INNER = 128
SUBLANES = 8
HEAD_ROWS = 32
HEAD_GROUP = 4
TAIL_ROWS = 64
TAIL_GROUP = 16
MIDDLE_ROWS = 8
AXES = ("fft", "grp")
BF16 = jnp.bfloat16
F32 = jnp.float32


def split(value):
    high = value.astype(BF16)
    return (high, (value - high.astype(F32)).astype(BF16))


def three_dot(left, right, dims):
    def one(x, y):
        return lax.dot_general(x, y, (dims, ((), ())), preferred_element_type=F32)

    return one(left[0], right[0]) + (one(left[1], right[0]) + one(left[0], right[1]))


def rotate(re, im, turn):
    num, den = turn
    num = num % den
    if num == 0:
        return (re, im)
    if 4 * num == den:
        return (-im, re)
    if 2 * num == den:
        return (-re, -im)
    if 4 * num == 3 * den:
        return (im, -re)
    if 8 * num == den:
        return ((re - im) * math.sqrt(0.5), (re + im) * math.sqrt(0.5))
    angle = 2.0 * math.pi * num / den
    cos, sin = (math.cos(angle), math.sin(angle))
    return (re * cos - im * sin, re * sin + im * cos)


def fft_list(values, sign):
    size = len(values)
    if size == 1:
        return values
    even = fft_list(values[0::2], sign)
    odd = fft_list(values[1::2], sign)
    low, high = ([], [])
    for k in range(size // 2):
        (er, ei), (r, i) = (even[k], odd[k])
        if 8 * k == size or 8 * k == 3 * size:
            root = math.sqrt(0.5)
            if 8 * k == size:
                tr, ti = ((r - sign * i) * root, (i + sign * r) * root)
            else:
                tr, ti = ((-r - sign * i) * root, (sign * r - i) * root)
            low.append((er + tr, ei + ti))
            high.append((er - tr, ei - ti))
        elif 4 * k == size:
            if sign > 0:
                low.append((er - i, ei + r))
                high.append((er + i, ei - r))
            else:
                low.append((er + i, ei - r))
                high.append((er - i, ei + r))
        else:
            tr, ti = rotate(r, i, (sign * k, size))
            low.append((er + tr, ei + ti))
            high.append((er - tr, ei - ti))
    return low + high


def times(x, y):
    return (x[0] * y[0] - x[1] * y[1], x[0] * y[1] + x[1] * y[0])


def times_conj(x, y):
    return (x[0] * y[0] + x[1] * y[1], x[1] * y[0] - x[0] * y[1])


def head_terms(src, own, outer, chunk, chunks):
    count = outer // chunks
    terms = []
    for r in range(count):
        re = im = None
        for s in range(chunks):
            at = (r + s * count) * INNER
            digit = src[own, at : at + INNER].astype(F32)
            if s == 0:
                re = digit
            else:
                angle = -2.0 * math.pi * s * (4 * chunk + 1) / (4 * chunks)
                re = re + digit * math.cos(angle)
                new = digit * math.sin(angle)
                im = new if im is None else im + new
        angle = -2.0 * math.pi * r * (4 * chunk + 1) / (4 * outer)
        cos, sin = (math.cos(angle), math.sin(angle))
        if im is None:
            terms.append((re * cos, re * sin))
        elif r == 0:
            terms.append((re, im))
        else:
            terms.append((re * cos - im * sin, re * sin + im * cos))
    return terms


def head_kernel(
    outer, classes, chunks, steps, devices, device_ref, a_ref, b_ref, out_ref, rows_ref, high_ref, low_ref, cos_ref, sin_ref
):
    step = pl.program_id(0)
    cols = rows_ref.shape[1] // 2
    count = outer // chunks
    pieces = devices // count
    each = INNER // pieces
    group = out_ref.shape[0] // pieces

    @pl.when(step == 0)
    def _():
        device = device_ref[0]
        high_ref[...], low_ref[...] = split(row_table(devices, device))
        for n, chunk in enumerate(classes):
            at = slice(n * count, (n + 1) * count)
            cos_ref[at, :], sin_ref[at, :] = row_turns(outer, devices, device, chunk, chunks)

    @pl.when(step < steps)
    def _():
        tile_rows = a_ref.shape[0]

        @pl.loop(0, tile_rows // SUBLANES)
        def _(i):
            own = pl.ds(pl.multiple_of(i * SUBLANES, SUBLANES), SUBLANES)
            for side, src in ((0, a_ref), (cols, b_ref)):
                at = pl.ds(pl.multiple_of(side + step * tile_rows + i * SUBLANES, SUBLANES), SUBLANES)
                for n, chunk in enumerate(classes):
                    result = fft_list(head_terms(src, own, outer, chunk, chunks), -1)
                    for e in range(count):
                        j = n * count + e
                        re, im = times_conj(result[e], (cos_ref[j : j + 1, :], sin_ref[j : j + 1, :]))
                        rows_ref[j, at, :INNER] = re
                        rows_ref[j, at, INNER:] = im

    @pl.when(step >= steps)
    def _():
        table = (high_ref[...], low_ref[...])

        @pl.loop(0, group)
        def _(g):
            j = (step - steps) * group + g
            if cols % INNER == 0:
                both = three_dot(table, split(rows_ref[j]), ((1,), (1,)))
                sides = (both[:, :cols], both[:, cols:])
            else:
                sides = tuple(
                    three_dot(table, split(rows_ref[j, at : at + cols]), ((1,), (1,))) for at in (0, cols)
                )
            for p in range(pieces):
                for at in (0, 1):
                    for part in (0, 1):
                        low = part * INNER + p * each
                        out_ref[g * pieces + p, 2 * at + part] = sides[at][low : low + each]


def head_stage(limbs_a, limbs_b, device, devices, classes, chunks):
    cols, length = limbs_a.shape
    outer = length // INNER
    count = outer // chunks
    pieces = devices // count
    tile_rows = min(cols, HEAD_ROWS)
    steps = cols // tile_rows
    group = math.gcd(count, HEAD_GROUP)
    blocks = count // group
    width = 2 * INNER
    total = len(classes) * count
    later = lambda i: jnp.maximum(i - steps, 0)
    in_spec = pl.BlockSpec((tile_rows, length), lambda i: (jnp.minimum(i, steps - 1), 0))
    out_spec = pl.BlockSpec(
        (group * pieces, None, 4, INNER // pieces, cols),
        lambda i: (later(i) % blocks, later(i) // blocks, 0, 0, 0),
    )
    return pl.pallas_call(
        functools.partial(head_kernel, outer, classes, chunks, steps, devices),
        grid=(steps + len(classes) * blocks,),
        in_specs=[pl.BlockSpec(memory_space=pltpu.SMEM), in_spec, in_spec],
        out_specs=out_spec,
        out_shape=jax.ShapeDtypeStruct((devices, len(classes), 4, INNER // pieces, cols), F32),
        scratch_shapes=[pltpu.VMEM((total, 2 * cols, width), F32)]
        + [pltpu.VMEM((width, width), BF16)] * 2
        + [pltpu.VMEM((total, INNER), F32)] * 2,
        cost_estimate=pl.CostEstimate(
            flops=12 * total * cols * width * width, bytes_accessed=16 * total * cols * width, transcendentals=0
        ),
        name="head_stage",
    )(device, limbs_a, limbs_b)


def middle_kernel(devices, x_ref, ka_cos, ka_sin, q_cos, q_sin, fh, fl, ih, il, v_ref, ya, yb):
    cols = x_ref.shape[3]
    rows = x_ref.shape[2]
    q_turn = (q_cos[...], q_sin[...])

    def turn_of(k):
        return times((ka_cos[k : k + 1, :], ka_sin[k : k + 1, :]), q_turn)

    for at, dst in ((0, ya), (2, yb)):
        result = fft_list([(x_ref[d, at], x_ref[d, at + 1]) for d in range(devices)], -1)
        for k in range(devices):
            re, im = times_conj(result[k], turn_of(k))
            dst[k * rows : (k + 1) * rows, :cols] = re
            dst[k * rows : (k + 1) * rows, cols:] = im
    forward = (fh[...], fl[...])
    inverse = (ih[...], il[...])
    a = three_dot(split(ya[...]), forward, ((1,), (0,)))
    b = three_dot(split(yb[...]), forward, ((1,), (0,)))
    re, im = times((a[:, :cols], a[:, cols:]), (b[:, :cols], b[:, cols:]))
    ya[:, :cols] = re
    ya[:, cols:] = im
    yb[...] = three_dot(split(ya[...]), inverse, ((1,), (0,)))
    terms = []
    for k in range(devices):
        part = slice(k * rows, (k + 1) * rows)
        terms.append(times((yb[part, :cols], yb[part, cols:]), turn_of(k)))
    result = fft_list(terms, 1)
    for d in range(devices):
        v_ref[d, 0] = result[d][0]
        v_ref[d, 1] = result[d][1]


def middle_stage(x, ka_cos, ka_sin, q_cos, q_sin, tables):
    devices, classes, _, count, cols = x.shape
    rows = MIDDLE_ROWS
    blocks = count // rows
    whole = lambda t: pl.BlockSpec(t.shape, lambda i: (0, 0))
    q_spec = pl.BlockSpec((rows, cols), lambda i: (i, 0))
    return pl.pallas_call(
        functools.partial(middle_kernel, devices),
        grid=(classes * blocks,),
        in_specs=[
            pl.BlockSpec((devices, None, 4, rows, cols), lambda i: (0, i // blocks, 0, i % blocks, 0)),
            whole(ka_cos),
            whole(ka_sin),
            q_spec,
            q_spec,
        ]
        + [whole(t) for t in tables],
        out_specs=pl.BlockSpec((devices, None, 2, rows, cols), lambda i: (0, i // blocks, 0, i % blocks, 0)),
        out_shape=jax.ShapeDtypeStruct((devices, classes, 2, count, cols), F32),
        scratch_shapes=[pltpu.VMEM((devices * rows, 2 * cols), F32)] * 2,
        cost_estimate=pl.CostEstimate(
            flops=36 * devices * classes * count * cols * cols * 4, bytes_accessed=24 * devices * classes * count * cols, transcendentals=0
        ),
        name="middle_stage",
    )(x, ka_cos, ka_sin, q_cos, q_sin, *tables)


def tail_kernel(outer, classes, chunks, steps, v_ref, table_ref, cos_ref, sin_ref, *refs):
    *others, out_ref, rows_ref, high_ref, low_ref = refs
    step = pl.program_id(0)
    _, cols, _ = rows_ref.shape
    count = outer // chunks
    pieces = INNER // v_ref.shape[2]
    block = v_ref.shape[0] // pieces
    group = min(block, 4)

    @pl.when(step == 0)
    def _():
        high_ref[...], low_ref[...] = split(table_ref[...])

    @pl.when(step < steps)
    def _():
        table = (high_ref[...], low_ref[...])

        @pl.loop(0, block // group)
        def _(i):
            def turned(g, part):
                own = [v_ref[(i * group + g) * pieces + p, part] for p in range(pieces)]
                return (own[0] if pieces == 1 else jnp.concatenate(own, axis=0)).T

            stacked = jnp.concatenate(
                [jnp.concatenate([turned(g, 0), turned(g, 1)], axis=1) for g in range(group)], axis=0
            )
            result = three_dot(split(stacked), table, ((1,), (0,)))
            for g in range(group):
                j = step * block + i * group + g
                part = result[g * cols : (g + 1) * cols]
                turn = (cos_ref[pl.ds(j, 1), :], sin_ref[pl.ds(j, 1), :])
                re, im = times((part[:, :INNER], part[:, INNER:]), turn)
                rows_ref[j, :, :INNER] = re
                rows_ref[j, :, INNER:] = im

    @pl.when(step >= steps)
    def _():
        tile_rows = out_ref.shape[-2]

        @pl.loop(0, tile_rows // SUBLANES)
        def _(i):
            own = pl.ds(pl.multiple_of(i * SUBLANES, SUBLANES), SUBLANES)
            at = pl.ds(pl.multiple_of((step - steps) * tile_rows + i * SUBLANES, SUBLANES), SUBLANES)
            mine = []
            for n, chunk in enumerate(classes):
                spectrum = [
                    (rows_ref[n * count + e, at, :INNER], rows_ref[n * count + e, at, INNER:]) for e in range(count)
                ]
                result = fft_list(spectrum, 1)
                mine.append([rotate(*result[r], (r * (4 * chunk + 1), 4 * outer)) for r in range(count)])
            for r in range(count):
                if out_ref.ndim == 3:
                    for n in range(len(classes)):
                        out_ref[n * count + r, own, :INNER] = mine[n][r][0]
                        out_ref[n * count + r, own, INNER:] = mine[n][r][1]
                    continue
                terms = []
                for o in others:
                    for n in range(o.shape[0] // count):
                        terms.append((o[n * count + r, own, :INNER], o[n * count + r, own, INNER:]))
                sums = fft_list(terms + [m[r] for m in mine], 1)
                for s in range(chunks):
                    re, im = rotate(*sums[s], (s, 4 * chunks))
                    low = (r + s * count) * INNER
                    high = low + outer * INNER
                    out_ref[own, low : low + INNER] = re
                    out_ref[own, high : high + INNER] = -im


def tail_stage(v, table, cos, sin, others, classes, chunks, outer):
    devices, _, _, each, cols = v.shape
    count = outer // chunks
    pieces = devices // count
    total = len(classes) * count
    block = math.gcd(count, TAIL_GROUP)
    blocks = count // block
    tile_rows = min(cols, TAIL_ROWS)
    width = 2 * INNER
    steps = len(classes) * blocks
    now = lambda i: jnp.minimum(i, steps - 1)
    later = lambda i: jnp.maximum(i - steps, 0)
    whole = lambda t: pl.BlockSpec(t.shape, lambda i: (0, 0))
    row_spec = lambda n: pl.BlockSpec((n, tile_rows, width), lambda i: (0, later(i), 0))
    if classes[-1] == chunks - 1:
        out_spec = pl.BlockSpec((tile_rows, outer * width), lambda i: (later(i), 0))
        out_shape = jax.ShapeDtypeStruct((cols, outer * width), F32)
    else:
        others = []
        out_spec = row_spec(total)
        out_shape = jax.ShapeDtypeStruct((total, cols, width), F32)
    return pl.pallas_call(
        functools.partial(tail_kernel, outer, classes, chunks, steps),
        grid=(steps + cols // tile_rows,),
        in_specs=[
            pl.BlockSpec((block * pieces, None, 2, each, cols), lambda i: (now(i) % blocks, now(i) // blocks, 0, 0, 0)),
            whole(table),
            whole(cos),
            whole(sin),
        ]
        + [row_spec(o.shape[0]) for o in others],
        out_specs=out_spec,
        out_shape=out_shape,
        scratch_shapes=[pltpu.VMEM((total, cols, width), F32)] + [pltpu.VMEM((width, width), BF16)] * 2,
        cost_estimate=pl.CostEstimate(
            flops=6 * total * cols * width * width, bytes_accessed=16 * total * cols * width, transcendentals=0
        ),
        name="tail_stage",
    )(v, table, cos, sin, *others)


def turns(phase, modulus):
    angle = (phase % modulus).astype(F32) * (2.0 * math.pi / modulus)
    return (jnp.cos(angle), jnp.sin(angle))


def iota(shape, dim):
    return lax.broadcasted_iota(jnp.int32, shape, dim)


def row_turns(outer, devices, device, chunk, chunks):
    shape = (outer // chunks, INNER)
    freq = chunks * iota(shape, 0) + chunk
    phase = (4 * freq + 1) * (devices * iota(shape, 1) + device)
    return turns(phase, 4 * outer * INNER * devices)


def row_table(devices, device):
    shape = (2 * INNER, 2 * INNER)
    row, col = (iota(shape, 0), iota(shape, 1))
    modulus = 4 * INNER * devices
    phase = 4 * (row % INNER) * (devices * (col % INNER) + device)
    quarter = INNER * devices * (row // INNER - col // INNER)
    angle = ((phase + quarter) % modulus).astype(F32) * (2.0 * math.pi / modulus)
    return jnp.cos(angle)


def spectral_turns(cols, devices, device, outer, classes, chunks, total):
    pieces = devices * chunks // outer
    each = INNER // pieces
    shape = (len(classes) * each, cols)
    row = iota(shape, 0)
    first = chunks * (device // pieces) + classes[0] + row // each
    inner = (device % pieces) * each + row % each
    return turns(iota(shape, 1) * (4 * (first + outer * inner) + 1), total)


def np_split(value):
    high = value.astype(np.float32).astype(BF16)
    low = (value - high.astype(np.float64)).astype(np.float32).astype(BF16)
    return (high, low)


def column_tables(cols, devices, scale):
    k = np.arange(devices)[:, None] * np.arange(cols)[None, :]
    angle = 2.0 * np.pi * k / (cols * devices)
    n = np.arange(cols)
    theta = 2.0 * np.pi * (n[:, None] * n[None, :] % cols) / cols
    forward = np.block([[np.cos(theta), -np.sin(theta)], [np.sin(theta), np.cos(theta)]])
    tables = np_split(forward) + np_split(forward.T * scale)
    return (np.cos(angle).astype(np.float32), np.sin(angle).astype(np.float32), tables)


def exchange(value):
    return lax.all_to_all(value, AXES, split_axis=0, concat_axis=0, tiled=True)


def on_device(limbs_a, limbs_b):
    devices = lax.axis_size(AXES)
    device = lax.axis_index(AXES)
    cols, length = limbs_a.shape
    outer = length // INNER
    total = length * cols * devices
    scale = 1.0 / (total * DIGIT_VAR * math.sqrt(total))
    chunks = max(1, 2 * outer // devices)
    groups = [list(range(1)), list(range(1, chunks))] if chunks > 1 else [[0]]
    ka_cos, ka_sin, tables = column_tables(cols, devices, scale)

    arrived = []
    for classes in groups:
        x = head_stage(limbs_a, limbs_b, device.reshape(1), devices, classes, chunks)
        arrived.append(exchange(x))
    back = []
    for x, classes in zip(arrived, groups):
        q_cos, q_sin = spectral_turns(cols, devices, device, outer, classes, chunks, 4 * total)
        back.append(exchange(middle_stage(x, ka_cos, ka_sin, q_cos, q_sin, tables)))
    table = row_table(devices, device)
    parts = []
    for v, classes in zip(back, groups):
        rows = [row_turns(outer, devices, device, h, chunks) for h in classes]
        cos, sin = (jnp.concatenate(r, axis=0) for r in zip(*rows))
        parts.append(tail_stage(v, table, cos, sin, parts, classes, chunks, outer))
    return parts[-1]


def solution(mesh):
    placed = P(AXES, None)
    return jax.shard_map(
        on_device, mesh=mesh, in_specs=(placed, placed), out_specs=placed, check_vma=False
    )
```

```python
import functools
import math

import jax
import jax.numpy as jnp
import numpy as np
from jax import lax
from jax.experimental import pallas as pl
from jax.experimental.pallas import tpu as pltpu
from jax.sharding import PartitionSpec as P

DIGIT_VAR = 5461.25
INNER = 128
SUBLANES = 8
HEAD_ROWS = 32
HEAD_GROUP = 4
TAIL_ROWS = 64
TAIL_GROUP = 16
MIDDLE_ROWS = 8
VMEM_BYTES = 67043328
AXES = ("fft", "grp")
BF16 = jnp.bfloat16
F32 = jnp.float32


def split(value):
    high = value.astype(BF16)
    return (high, (value - high.astype(F32)).astype(BF16))


def three_dot(left, right, dims):
    def one(x, y):
        return lax.dot_general(x, y, (dims, ((), ())), preferred_element_type=F32)

    return one(left[0], right[0]) + (one(left[1], right[0]) + one(left[0], right[1]))


def rotate(re, im, turn):
    num, den = turn
    num = num % den
    if num == 0:
        return (re, im)
    if 4 * num == den:
        return (-im, re)
    if 2 * num == den:
        return (-re, -im)
    if 4 * num == 3 * den:
        return (im, -re)
    if 8 * num == den:
        return ((re - im) * math.sqrt(0.5), (re + im) * math.sqrt(0.5))
    angle = 2.0 * math.pi * num / den
    cos, sin = (math.cos(angle), math.sin(angle))
    return (re * cos - im * sin, re * sin + im * cos)


def fft_list(values, sign):
    size = len(values)
    if size == 1:
        return values
    even = fft_list(values[0::2], sign)
    odd = fft_list(values[1::2], sign)
    low, high = ([], [])
    for k in range(size // 2):
        (er, ei), (r, i) = (even[k], odd[k])
        if 8 * k == size or 8 * k == 3 * size:
            root = math.sqrt(0.5)
            if 8 * k == size:
                tr, ti = ((r - sign * i) * root, (i + sign * r) * root)
            else:
                tr, ti = ((-r - sign * i) * root, (sign * r - i) * root)
            low.append((er + tr, ei + ti))
            high.append((er - tr, ei - ti))
        elif 4 * k == size:
            if sign > 0:
                low.append((er - i, ei + r))
                high.append((er + i, ei - r))
            else:
                low.append((er + i, ei - r))
                high.append((er - i, ei + r))
        else:
            tr, ti = rotate(r, i, (sign * k, size))
            low.append((er + tr, ei + ti))
            high.append((er - tr, ei - ti))
    return low + high


def times(x, y):
    return (x[0] * y[0] - x[1] * y[1], x[0] * y[1] + x[1] * y[0])


def times_conj(x, y):
    return (x[0] * y[0] + x[1] * y[1], x[1] * y[0] - x[0] * y[1])


def head_terms(src, own, outer, chunk, chunks):
    count = outer // chunks
    terms = []
    for r in range(count):
        re = im = None
        for s in range(chunks):
            at = (r + s * count) * INNER
            digit = src[own, at : at + INNER].astype(F32)
            if s == 0:
                re = digit
            else:
                angle = -2.0 * math.pi * s * (4 * chunk + 1) / (4 * chunks)
                re = re + digit * math.cos(angle)
                new = digit * math.sin(angle)
                im = new if im is None else im + new
        angle = -2.0 * math.pi * r * (4 * chunk + 1) / (4 * outer)
        cos, sin = (math.cos(angle), math.sin(angle))
        if im is None:
            terms.append((re * cos, re * sin))
        elif r == 0:
            terms.append((re, im))
        else:
            terms.append((re * cos - im * sin, re * sin + im * cos))
    return terms


def head_kernel(
    outer, classes, chunks, steps, devices, device_ref, a_ref, b_ref, out_ref, rows_ref, high_ref, low_ref, cos_ref, sin_ref
):
    step = pl.program_id(0)
    cols = rows_ref.shape[1] // 2
    count = outer // chunks
    pieces = devices // count
    each = INNER // pieces
    group = out_ref.shape[0] // pieces

    @pl.when(step == 0)
    def _():
        device = device_ref[0]
        high_ref[...], low_ref[...] = split(row_table(devices, device))
        for n, chunk in enumerate(classes):
            at = slice(n * count, (n + 1) * count)
            cos_ref[at, :], sin_ref[at, :] = row_turns(outer, devices, device, chunk, chunks)

    @pl.when(step < steps)
    def _():
        tile_rows = a_ref.shape[0]

        @pl.loop(0, tile_rows // SUBLANES)
        def _(i):
            own = pl.ds(pl.multiple_of(i * SUBLANES, SUBLANES), SUBLANES)
            for side, src in ((0, a_ref), (cols, b_ref)):
                at = pl.ds(pl.multiple_of(side + step * tile_rows + i * SUBLANES, SUBLANES), SUBLANES)
                for n, chunk in enumerate(classes):
                    result = fft_list(head_terms(src, own, outer, chunk, chunks), -1)
                    for e in range(count):
                        j = n * count + e
                        re, im = times_conj(result[e], (cos_ref[j : j + 1, :], sin_ref[j : j + 1, :]))
                        rows_ref[j, at, :INNER] = re
                        rows_ref[j, at, INNER:] = im

    @pl.when(step >= steps)
    def _():
        table = (high_ref[...], low_ref[...])

        @pl.loop(0, group)
        def _(g):
            j = (step - steps) * group + g
            if cols % INNER == 0:
                both = three_dot(table, split(rows_ref[j]), ((1,), (1,)))
                sides = (both[:, :cols], both[:, cols:])
            else:
                sides = tuple(
                    three_dot(table, split(rows_ref[j, at : at + cols]), ((1,), (1,))) for at in (0, cols)
                )
            for p in range(pieces):
                for at in (0, 1):
                    for part in (0, 1):
                        low = part * INNER + p * each
                        out_ref[g * pieces + p, 2 * at + part] = sides[at][low : low + each]


def head_stage(limbs_a, limbs_b, device, devices, classes, chunks):
    cols, length = limbs_a.shape
    outer = length // INNER
    count = outer // chunks
    pieces = devices // count
    tile_rows = min(cols, HEAD_ROWS)
    steps = cols // tile_rows
    group = math.gcd(count, HEAD_GROUP)
    blocks = count // group
    width = 2 * INNER
    total = len(classes) * count
    later = lambda i: jnp.maximum(i - steps, 0)
    in_spec = pl.BlockSpec((tile_rows, length), lambda i: (jnp.minimum(i, steps - 1), 0))
    out_spec = pl.BlockSpec(
        (group * pieces, None, 4, INNER // pieces, cols),
        lambda i: (later(i) % blocks, later(i) // blocks, 0, 0, 0),
    )
    return pl.pallas_call(
        functools.partial(head_kernel, outer, classes, chunks, steps, devices),
        grid=(steps + len(classes) * blocks,),
        in_specs=[pl.BlockSpec(memory_space=pltpu.SMEM), in_spec, in_spec],
        out_specs=out_spec,
        out_shape=jax.ShapeDtypeStruct((devices, len(classes), 4, INNER // pieces, cols), F32),
        scratch_shapes=[pltpu.VMEM((total, 2 * cols, width), F32)]
        + [pltpu.VMEM((width, width), BF16)] * 2
        + [pltpu.VMEM((total, INNER), F32)] * 2,
        cost_estimate=pl.CostEstimate(
            flops=12 * total * cols * width * width, bytes_accessed=16 * total * cols * width, transcendentals=0
        ),
        compiler_params=pltpu.CompilerParams(vmem_limit_bytes=VMEM_BYTES),
        name="head_stage",
    )(device, limbs_a, limbs_b)


def middle_kernel(devices, x_ref, ka_cos, ka_sin, q_cos, q_sin, fh, fl, ih, il, v_ref, ya, yb):
    cols = x_ref.shape[3]
    rows = x_ref.shape[2]
    q_turn = (q_cos[...], q_sin[...])

    def turn_of(k):
        return times((ka_cos[k : k + 1, :], ka_sin[k : k + 1, :]), q_turn)

    for at, dst in ((0, ya), (2, yb)):
        result = fft_list([(x_ref[d, at], x_ref[d, at + 1]) for d in range(devices)], -1)
        for k in range(devices):
            re, im = times_conj(result[k], turn_of(k))
            dst[k * rows : (k + 1) * rows, :cols] = re
            dst[k * rows : (k + 1) * rows, cols:] = im
    forward = (fh[...], fl[...])
    inverse = (ih[...], il[...])
    a = three_dot(split(ya[...]), forward, ((1,), (0,)))
    b = three_dot(split(yb[...]), forward, ((1,), (0,)))
    re, im = times((a[:, :cols], a[:, cols:]), (b[:, :cols], b[:, cols:]))
    ya[:, :cols] = re
    ya[:, cols:] = im
    yb[...] = three_dot(split(ya[...]), inverse, ((1,), (0,)))
    terms = []
    for k in range(devices):
        part = slice(k * rows, (k + 1) * rows)
        terms.append(times((yb[part, :cols], yb[part, cols:]), turn_of(k)))
    result = fft_list(terms, 1)
    for d in range(devices):
        v_ref[d, 0] = result[d][0]
        v_ref[d, 1] = result[d][1]


def middle_stage(x, ka_cos, ka_sin, q_cos, q_sin, tables):
    devices, classes, _, count, cols = x.shape
    rows = MIDDLE_ROWS
    blocks = count // rows
    whole = lambda t: pl.BlockSpec(t.shape, lambda i: (0, 0))
    q_spec = pl.BlockSpec((rows, cols), lambda i: (i, 0))
    return pl.pallas_call(
        functools.partial(middle_kernel, devices),
        grid=(classes * blocks,),
        in_specs=[
            pl.BlockSpec((devices, None, 4, rows, cols), lambda i: (0, i // blocks, 0, i % blocks, 0)),
            whole(ka_cos),
            whole(ka_sin),
            q_spec,
            q_spec,
        ]
        + [whole(t) for t in tables],
        out_specs=pl.BlockSpec((devices, None, 2, rows, cols), lambda i: (0, i // blocks, 0, i % blocks, 0)),
        out_shape=jax.ShapeDtypeStruct((devices, classes, 2, count, cols), F32),
        scratch_shapes=[pltpu.VMEM((devices * rows, 2 * cols), F32)] * 2,
        cost_estimate=pl.CostEstimate(
            flops=36 * devices * classes * count * cols * cols * 4, bytes_accessed=24 * devices * classes * count * cols, transcendentals=0
        ),
        compiler_params=pltpu.CompilerParams(vmem_limit_bytes=VMEM_BYTES),
        name="middle_stage",
    )(x, ka_cos, ka_sin, q_cos, q_sin, *tables)


def tail_kernel(outer, classes, chunks, steps, v_ref, table_ref, cos_ref, sin_ref, *refs):
    *others, out_ref, rows_ref, high_ref, low_ref = refs
    step = pl.program_id(0)
    _, cols, _ = rows_ref.shape
    count = outer // chunks
    pieces = INNER // v_ref.shape[2]
    block = v_ref.shape[0] // pieces
    group = min(block, 4)

    @pl.when(step == 0)
    def _():
        high_ref[...], low_ref[...] = split(table_ref[...])

    @pl.when(step < steps)
    def _():
        table = (high_ref[...], low_ref[...])

        @pl.loop(0, block // group)
        def _(i):
            def turned(g, part):
                own = [v_ref[(i * group + g) * pieces + p, part] for p in range(pieces)]
                return (own[0] if pieces == 1 else jnp.concatenate(own, axis=0)).T

            stacked = jnp.concatenate(
                [jnp.concatenate([turned(g, 0), turned(g, 1)], axis=1) for g in range(group)], axis=0
            )
            result = three_dot(split(stacked), table, ((1,), (0,)))
            for g in range(group):
                j = step * block + i * group + g
                part = result[g * cols : (g + 1) * cols]
                turn = (cos_ref[pl.ds(j, 1), :], sin_ref[pl.ds(j, 1), :])
                re, im = times((part[:, :INNER], part[:, INNER:]), turn)
                rows_ref[j, :, :INNER] = re
                rows_ref[j, :, INNER:] = im

    @pl.when(step >= steps)
    def _():
        tile_rows = out_ref.shape[-2]

        @pl.loop(0, tile_rows // SUBLANES)
        def _(i):
            own = pl.ds(pl.multiple_of(i * SUBLANES, SUBLANES), SUBLANES)
            at = pl.ds(pl.multiple_of((step - steps) * tile_rows + i * SUBLANES, SUBLANES), SUBLANES)
            mine = []
            for n, chunk in enumerate(classes):
                spectrum = [
                    (rows_ref[n * count + e, at, :INNER], rows_ref[n * count + e, at, INNER:]) for e in range(count)
                ]
                result = fft_list(spectrum, 1)
                mine.append([rotate(*result[r], (r * (4 * chunk + 1), 4 * outer)) for r in range(count)])
            for r in range(count):
                if out_ref.ndim == 3:
                    for n in range(len(classes)):
                        out_ref[n * count + r, own, :INNER] = mine[n][r][0]
                        out_ref[n * count + r, own, INNER:] = mine[n][r][1]
                    continue
                terms = []
                for o in others:
                    for n in range(o.shape[0] // count):
                        terms.append((o[n * count + r, own, :INNER], o[n * count + r, own, INNER:]))
                sums = fft_list(terms + [m[r] for m in mine], 1)
                for s in range(chunks):
                    re, im = rotate(*sums[s], (s, 4 * chunks))
                    low = (r + s * count) * INNER
                    high = low + outer * INNER
                    out_ref[own, low : low + INNER] = re
                    out_ref[own, high : high + INNER] = -im


def tail_stage(v, table, cos, sin, others, classes, chunks, outer):
    devices, _, _, each, cols = v.shape
    count = outer // chunks
    pieces = devices // count
    total = len(classes) * count
    block = math.gcd(count, TAIL_GROUP)
    blocks = count // block
    tile_rows = min(cols, TAIL_ROWS)
    width = 2 * INNER
    steps = len(classes) * blocks
    now = lambda i: jnp.minimum(i, steps - 1)
    later = lambda i: jnp.maximum(i - steps, 0)
    whole = lambda t: pl.BlockSpec(t.shape, lambda i: (0, 0))
    row_spec = lambda n: pl.BlockSpec((n, tile_rows, width), lambda i: (0, later(i), 0))
    if classes[-1] == chunks - 1:
        out_spec = pl.BlockSpec((tile_rows, outer * width), lambda i: (later(i), 0))
        out_shape = jax.ShapeDtypeStruct((cols, outer * width), F32)
    else:
        others = []
        out_spec = row_spec(total)
        out_shape = jax.ShapeDtypeStruct((total, cols, width), F32)
    return pl.pallas_call(
        functools.partial(tail_kernel, outer, classes, chunks, steps),
        grid=(steps + cols // tile_rows,),
        in_specs=[
            pl.BlockSpec((block * pieces, None, 2, each, cols), lambda i: (now(i) % blocks, now(i) // blocks, 0, 0, 0)),
            whole(table),
            whole(cos),
            whole(sin),
        ]
        + [row_spec(o.shape[0]) for o in others],
        out_specs=out_spec,
        out_shape=out_shape,
        scratch_shapes=[pltpu.VMEM((total, cols, width), F32)] + [pltpu.VMEM((width, width), BF16)] * 2,
        cost_estimate=pl.CostEstimate(
            flops=6 * total * cols * width * width, bytes_accessed=16 * total * cols * width, transcendentals=0
        ),
        compiler_params=pltpu.CompilerParams(vmem_limit_bytes=VMEM_BYTES),
        name="tail_stage",
    )(v, table, cos, sin, *others)


def turns(phase, modulus):
    angle = (phase & (modulus - 1)).astype(F32) * (2.0 * math.pi / modulus)
    return (jnp.cos(angle), jnp.sin(angle))


def iota(shape, dim):
    return lax.broadcasted_iota(jnp.int32, shape, dim)


def row_turns(outer, devices, device, chunk, chunks):
    shape = (outer // chunks, INNER)
    freq = chunks * iota(shape, 0) + chunk
    phase = (4 * freq + 1) * (devices * iota(shape, 1) + device)
    return turns(phase, 4 * outer * INNER * devices)


def row_table(devices, device):
    shape = (2 * INNER, 2 * INNER)
    row, col = (iota(shape, 0), iota(shape, 1))
    modulus = 4 * INNER * devices
    mask = INNER - 1
    phase = 4 * (row & mask) * (devices * (col & mask) + device)
    quarter = devices * ((row & INNER) - (col & INNER))
    angle = ((phase + quarter) & (modulus - 1)).astype(F32) * (2.0 * math.pi / modulus)
    return jnp.cos(angle)


def spectral_turns(cols, devices, device, outer, classes, chunks, total):
    pieces = devices * chunks // outer
    each = INNER // pieces
    shape = (len(classes) * each, cols)
    row = iota(shape, 0)
    first = chunks * (device // pieces) + classes[0] + row // each
    inner = (device % pieces) * each + row % each
    return turns(iota(shape, 1) * (4 * (first + outer * inner) + 1), total)


def np_split(value):
    high = value.astype(np.float32).astype(BF16)
    low = (value - high.astype(np.float64)).astype(np.float32).astype(BF16)
    return (high, low)


def column_tables(cols, devices, scale):
    k = np.arange(devices)[:, None] * np.arange(cols)[None, :]
    angle = 2.0 * np.pi * k / (cols * devices)
    n = np.arange(cols)
    theta = 2.0 * np.pi * (n[:, None] * n[None, :] % cols) / cols
    forward = np.block([[np.cos(theta), -np.sin(theta)], [np.sin(theta), np.cos(theta)]])
    tables = np_split(forward) + np_split(forward.T * scale)
    return (np.cos(angle).astype(np.float32), np.sin(angle).astype(np.float32), tables)


def exchange(value):
    return lax.all_to_all(value, AXES, split_axis=0, concat_axis=0, tiled=True)


def on_device(limbs_a, limbs_b):
    devices = lax.axis_size(AXES)
    device = lax.axis_index(AXES)
    cols, length = limbs_a.shape
    outer = length // INNER
    total = length * cols * devices
    scale = 1.0 / (total * DIGIT_VAR * math.sqrt(total))
    chunks = max(1, 2 * outer // devices)
    groups = [list(range(1)), list(range(1, chunks))] if chunks > 1 else [[0]]
    ka_cos, ka_sin, tables = column_tables(cols, devices, scale)

    arrived = []
    for classes in groups:
        x = head_stage(limbs_a, limbs_b, device.reshape(1), devices, classes, chunks)
        arrived.append(exchange(x))
    back = []
    for x, classes in zip(arrived, groups):
        q_cos, q_sin = spectral_turns(cols, devices, device, outer, classes, chunks, 4 * total)
        back.append(exchange(middle_stage(x, ka_cos, ka_sin, q_cos, q_sin, tables)))
    table = row_table(devices, device)
    parts = []
    for v, classes in zip(back, groups):
        rows = [row_turns(outer, devices, device, h, chunks) for h in classes]
        cos, sin = (jnp.concatenate(r, axis=0) for r in zip(*rows))
        parts.append(tail_stage(v, table, cos, sin, parts, classes, chunks, outer))
    return parts[-1]


def solution(mesh):
    placed = P(AXES, None)
    return jax.shard_map(
        on_device, mesh=mesh, in_specs=(placed, placed), out_specs=placed, check_vma=False
    )
```

```python
import functools
import math

import jax
import jax.numpy as jnp
import numpy as np
from jax import lax
from jax.experimental import pallas as pl
from jax.experimental.pallas import tpu as pltpu
from jax.sharding import PartitionSpec as P

DIGIT_VAR = 5461.25
INNER = 128
SUBLANES = 8
HEAD_ROWS = 32
HEAD_GROUP = 4
TAIL_ROWS = 64
TAIL_GROUP = 16
MIDDLE_ROWS = 8
VMEM_BYTES = 67043328
AXES = ("fft", "grp")
BF16 = jnp.bfloat16
F32 = jnp.float32


def split(value):
    high = value.astype(BF16)
    return (high, (value - high.astype(F32)).astype(BF16))


def three_dot(left, right, dims):
    def one(x, y):
        return lax.dot_general(x, y, (dims, ((), ())), preferred_element_type=F32)

    return one(left[0], right[0]) + (one(left[1], right[0]) + one(left[0], right[1]))


def rotate(re, im, turn):
    num, den = turn
    num = num % den
    if num == 0:
        return (re, im)
    if 4 * num == den:
        return (-im, re)
    if 2 * num == den:
        return (-re, -im)
    if 4 * num == 3 * den:
        return (im, -re)
    if 8 * num == den:
        return ((re - im) * math.sqrt(0.5), (re + im) * math.sqrt(0.5))
    angle = 2.0 * math.pi * num / den
    cos, sin = (math.cos(angle), math.sin(angle))
    return (re * cos - im * sin, re * sin + im * cos)


def fft_list(values, sign):
    size = len(values)
    if size == 1:
        return values
    even = fft_list(values[0::2], sign)
    odd = fft_list(values[1::2], sign)
    low, high = ([], [])
    for k in range(size // 2):
        (er, ei), (r, i) = (even[k], odd[k])
        if 8 * k == size or 8 * k == 3 * size:
            root = math.sqrt(0.5)
            if 8 * k == size:
                tr, ti = ((r - sign * i) * root, (i + sign * r) * root)
            else:
                tr, ti = ((-r - sign * i) * root, (sign * r - i) * root)
            low.append((er + tr, ei + ti))
            high.append((er - tr, ei - ti))
        elif 4 * k == size:
            if sign > 0:
                low.append((er - i, ei + r))
                high.append((er + i, ei - r))
            else:
                low.append((er + i, ei - r))
                high.append((er - i, ei + r))
        else:
            tr, ti = rotate(r, i, (sign * k, size))
            low.append((er + tr, ei + ti))
            high.append((er - tr, ei - ti))
    return low + high


def times(x, y):
    return (x[0] * y[0] - x[1] * y[1], x[0] * y[1] + x[1] * y[0])


def times_conj(x, y):
    return (x[0] * y[0] + x[1] * y[1], x[1] * y[0] - x[0] * y[1])


def head_terms(src, own, outer, chunk, chunks):
    count = outer // chunks
    terms = []
    for r in range(count):
        re = im = None
        for s in range(chunks):
            at = (r + s * count) * INNER
            digit = src[own, at : at + INNER].astype(F32)
            if s == 0:
                re = digit
            else:
                angle = -2.0 * math.pi * s * (4 * chunk + 1) / (4 * chunks)
                re = re + digit * math.cos(angle)
                new = digit * math.sin(angle)
                im = new if im is None else im + new
        angle = -2.0 * math.pi * r * (4 * chunk + 1) / (4 * outer)
        cos, sin = (math.cos(angle), math.sin(angle))
        if im is None:
            terms.append((re * cos, re * sin))
        elif r == 0:
            terms.append((re, im))
        else:
            terms.append((re * cos - im * sin, re * sin + im * cos))
    return terms


def head_kernel(
    outer, classes, chunks, steps, devices, device_ref, a_ref, b_ref, out_ref, rows_ref, high_ref, low_ref, cos_ref, sin_ref
):
    step = pl.program_id(0)
    cols = rows_ref.shape[1] // 2
    count = outer // chunks
    pieces = devices // count
    each = INNER // pieces
    group = out_ref.shape[0] // pieces

    @pl.when(step == 0)
    def _():
        device = device_ref[0]
        high_ref[...], low_ref[...] = split(row_table(devices, device))
        for n, chunk in enumerate(classes):
            at = slice(n * count, (n + 1) * count)
            cos_ref[at, :], sin_ref[at, :] = row_turns(outer, devices, device, chunk, chunks)

    @pl.when(step < steps)
    def _():
        tile_rows = a_ref.shape[0]

        @pl.loop(0, tile_rows // SUBLANES, unroll=2)
        def _(i):
            own = pl.ds(pl.multiple_of(i * SUBLANES, SUBLANES), SUBLANES)
            for side, src in ((0, a_ref), (cols, b_ref)):
                at = pl.ds(pl.multiple_of(side + step * tile_rows + i * SUBLANES, SUBLANES), SUBLANES)
                for n, chunk in enumerate(classes):
                    result = fft_list(head_terms(src, own, outer, chunk, chunks), -1)
                    for e in range(count):
                        j = n * count + e
                        re, im = times_conj(result[e], (cos_ref[j : j + 1, :], sin_ref[j : j + 1, :]))
                        rows_ref[j, at, :INNER] = re
                        rows_ref[j, at, INNER:] = im

    @pl.when(step >= steps)
    def _():
        table = (high_ref[...], low_ref[...])

        @pl.loop(0, group, unroll=4)
        def _(g):
            j = (step - steps) * group + g
            if cols % INNER == 0:
                both = three_dot(table, split(rows_ref[j]), ((1,), (1,)))
                sides = (both[:, :cols], both[:, cols:])
            else:
                sides = tuple(
                    three_dot(table, split(rows_ref[j, at : at + cols]), ((1,), (1,))) for at in (0, cols)
                )
            for p in range(pieces):
                for at in (0, 1):
                    for part in (0, 1):
                        low = part * INNER + p * each
                        out_ref[g * pieces + p, 2 * at + part] = sides[at][low : low + each]


def head_stage(limbs_a, limbs_b, device, devices, classes, chunks):
    cols, length = limbs_a.shape
    outer = length // INNER
    count = outer // chunks
    pieces = devices // count
    tile_rows = min(cols, HEAD_ROWS)
    steps = cols // tile_rows
    group = math.gcd(count, HEAD_GROUP)
    blocks = count // group
    width = 2 * INNER
    total = len(classes) * count
    later = lambda i: jnp.maximum(i - steps, 0)
    in_spec = pl.BlockSpec((tile_rows, length), lambda i: (jnp.minimum(i, steps - 1), 0))
    out_spec = pl.BlockSpec(
        (group * pieces, None, 4, INNER // pieces, cols),
        lambda i: (later(i) % blocks, later(i) // blocks, 0, 0, 0),
    )
    return pl.pallas_call(
        functools.partial(head_kernel, outer, classes, chunks, steps, devices),
        grid=(steps + len(classes) * blocks,),
        in_specs=[pl.BlockSpec(memory_space=pltpu.SMEM), in_spec, in_spec],
        out_specs=out_spec,
        out_shape=jax.ShapeDtypeStruct((devices, len(classes), 4, INNER // pieces, cols), F32),
        scratch_shapes=[pltpu.VMEM((total, 2 * cols, width), F32)]
        + [pltpu.VMEM((width, width), BF16)] * 2
        + [pltpu.VMEM((total, INNER), F32)] * 2,
        cost_estimate=pl.CostEstimate(
            flops=12 * total * cols * width * width, bytes_accessed=16 * total * cols * width, transcendentals=0
        ),
        compiler_params=pltpu.CompilerParams(vmem_limit_bytes=VMEM_BYTES),
        name="head_stage",
    )(device, limbs_a, limbs_b)


def middle_kernel(devices, x_ref, ka_cos, ka_sin, q_cos, q_sin, fh, fl, ih, il, v_ref, ya, yb):
    cols = x_ref.shape[3]
    rows = x_ref.shape[2]
    q_turn = (q_cos[...], q_sin[...])

    def turn_of(k):
        return times((ka_cos[k : k + 1, :], ka_sin[k : k + 1, :]), q_turn)

    for at, dst in ((0, ya), (2, yb)):
        result = fft_list([(x_ref[d, at], x_ref[d, at + 1]) for d in range(devices)], -1)
        for k in range(devices):
            re, im = times_conj(result[k], turn_of(k))
            dst[k * rows : (k + 1) * rows, :cols] = re
            dst[k * rows : (k + 1) * rows, cols:] = im
    forward = (fh[...], fl[...])
    inverse = (ih[...], il[...])
    a = three_dot(split(ya[...]), forward, ((1,), (0,)))
    b = three_dot(split(yb[...]), forward, ((1,), (0,)))
    re, im = times((a[:, :cols], a[:, cols:]), (b[:, :cols], b[:, cols:]))
    ya[:, :cols] = re
    ya[:, cols:] = im
    yb[...] = three_dot(split(ya[...]), inverse, ((1,), (0,)))
    terms = []
    for k in range(devices):
        part = slice(k * rows, (k + 1) * rows)
        terms.append(times((yb[part, :cols], yb[part, cols:]), turn_of(k)))
    result = fft_list(terms, 1)
    for d in range(devices):
        v_ref[d, 0] = result[d][0]
        v_ref[d, 1] = result[d][1]


def middle_stage(x, ka_cos, ka_sin, q_cos, q_sin, tables):
    devices, classes, _, count, cols = x.shape
    rows = MIDDLE_ROWS
    blocks = count // rows
    whole = lambda t: pl.BlockSpec(t.shape, lambda i: (0, 0))
    q_spec = pl.BlockSpec((rows, cols), lambda i: (i, 0))
    return pl.pallas_call(
        functools.partial(middle_kernel, devices),
        grid=(classes * blocks,),
        in_specs=[
            pl.BlockSpec((devices, None, 4, rows, cols), lambda i: (0, i // blocks, 0, i % blocks, 0)),
            whole(ka_cos),
            whole(ka_sin),
            q_spec,
            q_spec,
        ]
        + [whole(t) for t in tables],
        out_specs=pl.BlockSpec((devices, None, 2, rows, cols), lambda i: (0, i // blocks, 0, i % blocks, 0)),
        out_shape=jax.ShapeDtypeStruct((devices, classes, 2, count, cols), F32),
        scratch_shapes=[pltpu.VMEM((devices * rows, 2 * cols), F32)] * 2,
        cost_estimate=pl.CostEstimate(
            flops=36 * devices * classes * count * cols * cols * 4, bytes_accessed=24 * devices * classes * count * cols, transcendentals=0
        ),
        compiler_params=pltpu.CompilerParams(vmem_limit_bytes=VMEM_BYTES),
        name="middle_stage",
    )(x, ka_cos, ka_sin, q_cos, q_sin, *tables)


def tail_kernel(outer, classes, chunks, steps, v_ref, table_ref, cos_ref, sin_ref, *refs):
    *others, out_ref, rows_ref, high_ref, low_ref = refs
    step = pl.program_id(0)
    _, cols, _ = rows_ref.shape
    count = outer // chunks
    pieces = INNER // v_ref.shape[2]
    block = v_ref.shape[0] // pieces
    group = min(block, 4)

    @pl.when(step == 0)
    def _():
        high_ref[...], low_ref[...] = split(table_ref[...])

    @pl.when(step < steps)
    def _():
        table = (high_ref[...], low_ref[...])

        @pl.loop(0, block // group, unroll=4)
        def _(i):
            def turned(g, part):
                own = [v_ref[(i * group + g) * pieces + p, part] for p in range(pieces)]
                return (own[0] if pieces == 1 else jnp.concatenate(own, axis=0)).T

            stacked = jnp.concatenate(
                [jnp.concatenate([turned(g, 0), turned(g, 1)], axis=1) for g in range(group)], axis=0
            )
            result = three_dot(split(stacked), table, ((1,), (0,)))
            for g in range(group):
                j = step * block + i * group + g
                part = result[g * cols : (g + 1) * cols]
                turn = (cos_ref[pl.ds(j, 1), :], sin_ref[pl.ds(j, 1), :])
                re, im = times((part[:, :INNER], part[:, INNER:]), turn)
                rows_ref[j, :, :INNER] = re
                rows_ref[j, :, INNER:] = im

    @pl.when(step >= steps)
    def _():
        tile_rows = out_ref.shape[-2]

        @pl.loop(0, tile_rows // SUBLANES, unroll=2)
        def _(i):
            own = pl.ds(pl.multiple_of(i * SUBLANES, SUBLANES), SUBLANES)
            at = pl.ds(pl.multiple_of((step - steps) * tile_rows + i * SUBLANES, SUBLANES), SUBLANES)
            mine = []
            for n, chunk in enumerate(classes):
                spectrum = [
                    (rows_ref[n * count + e, at, :INNER], rows_ref[n * count + e, at, INNER:]) for e in range(count)
                ]
                result = fft_list(spectrum, 1)
                mine.append([rotate(*result[r], (r * (4 * chunk + 1), 4 * outer)) for r in range(count)])
            for r in range(count):
                if out_ref.ndim == 3:
                    for n in range(len(classes)):
                        out_ref[n * count + r, own, :INNER] = mine[n][r][0]
                        out_ref[n * count + r, own, INNER:] = mine[n][r][1]
                    continue
                terms = []
                for o in others:
                    for n in range(o.shape[0] // count):
                        terms.append((o[n * count + r, own, :INNER], o[n * count + r, own, INNER:]))
                sums = fft_list(terms + [m[r] for m in mine], 1)
                for s in range(chunks):
                    re, im = rotate(*sums[s], (s, 4 * chunks))
                    low = (r + s * count) * INNER
                    high = low + outer * INNER
                    out_ref[own, low : low + INNER] = re
                    out_ref[own, high : high + INNER] = -im


def tail_stage(v, table, cos, sin, others, classes, chunks, outer):
    devices, _, _, each, cols = v.shape
    count = outer // chunks
    pieces = devices // count
    total = len(classes) * count
    block = math.gcd(count, TAIL_GROUP)
    blocks = count // block
    tile_rows = min(cols, TAIL_ROWS)
    width = 2 * INNER
    steps = len(classes) * blocks
    now = lambda i: jnp.minimum(i, steps - 1)
    later = lambda i: jnp.maximum(i - steps, 0)
    whole = lambda t: pl.BlockSpec(t.shape, lambda i: (0, 0))
    row_spec = lambda n: pl.BlockSpec((n, tile_rows, width), lambda i: (0, later(i), 0))
    if classes[-1] == chunks - 1:
        out_spec = pl.BlockSpec((tile_rows, outer * width), lambda i: (later(i), 0))
        out_shape = jax.ShapeDtypeStruct((cols, outer * width), F32)
    else:
        others = []
        out_spec = row_spec(total)
        out_shape = jax.ShapeDtypeStruct((total, cols, width), F32)
    return pl.pallas_call(
        functools.partial(tail_kernel, outer, classes, chunks, steps),
        grid=(steps + cols // tile_rows,),
        in_specs=[
            pl.BlockSpec((block * pieces, None, 2, each, cols), lambda i: (now(i) % blocks, now(i) // blocks, 0, 0, 0)),
            whole(table),
            whole(cos),
            whole(sin),
        ]
        + [row_spec(o.shape[0]) for o in others],
        out_specs=out_spec,
        out_shape=out_shape,
        scratch_shapes=[pltpu.VMEM((total, cols, width), F32)] + [pltpu.VMEM((width, width), BF16)] * 2,
        cost_estimate=pl.CostEstimate(
            flops=6 * total * cols * width * width, bytes_accessed=16 * total * cols * width, transcendentals=0
        ),
        compiler_params=pltpu.CompilerParams(vmem_limit_bytes=VMEM_BYTES),
        name="tail_stage",
    )(v, table, cos, sin, *others)


def turns(phase, modulus):
    angle = (phase & (modulus - 1)).astype(F32) * (2.0 * math.pi / modulus)
    return (jnp.cos(angle), jnp.sin(angle))


def iota(shape, dim):
    return lax.broadcasted_iota(jnp.int32, shape, dim)


def row_turns(outer, devices, device, chunk, chunks):
    shape = (outer // chunks, INNER)
    freq = chunks * iota(shape, 0) + chunk
    phase = (4 * freq + 1) * (devices * iota(shape, 1) + device)
    return turns(phase, 4 * outer * INNER * devices)


def row_table(devices, device):
    shape = (2 * INNER, 2 * INNER)
    row, col = (iota(shape, 0), iota(shape, 1))
    modulus = 4 * INNER * devices
    mask = INNER - 1
    phase = 4 * (row & mask) * (devices * (col & mask) + device)
    quarter = devices * ((row & INNER) - (col & INNER))
    angle = ((phase + quarter) & (modulus - 1)).astype(F32) * (2.0 * math.pi / modulus)
    return jnp.cos(angle)


def spectral_turns(cols, devices, device, outer, classes, chunks, total):
    pieces = devices * chunks // outer
    each = INNER // pieces
    shape = (len(classes) * each, cols)
    row = iota(shape, 0)
    first = chunks * (device // pieces) + classes[0] + row // each
    inner = (device % pieces) * each + row % each
    return turns(iota(shape, 1) * (4 * (first + outer * inner) + 1), total)


def np_split(value):
    high = value.astype(np.float32).astype(BF16)
    low = (value - high.astype(np.float64)).astype(np.float32).astype(BF16)
    return (high, low)


def column_tables(cols, devices, scale):
    k = np.arange(devices)[:, None] * np.arange(cols)[None, :]
    angle = 2.0 * np.pi * k / (cols * devices)
    n = np.arange(cols)
    theta = 2.0 * np.pi * (n[:, None] * n[None, :] % cols) / cols
    forward = np.block([[np.cos(theta), -np.sin(theta)], [np.sin(theta), np.cos(theta)]])
    tables = np_split(forward) + np_split(forward.T * scale)
    return (np.cos(angle).astype(np.float32), np.sin(angle).astype(np.float32), tables)


def exchange(value):
    return lax.all_to_all(value, AXES, split_axis=0, concat_axis=0, tiled=True)


def on_device(limbs_a, limbs_b):
    devices = lax.axis_size(AXES)
    device = lax.axis_index(AXES)
    cols, length = limbs_a.shape
    outer = length // INNER
    total = length * cols * devices
    scale = 1.0 / (total * DIGIT_VAR * math.sqrt(total))
    chunks = max(1, 2 * outer // devices)
    groups = [list(range(1)), list(range(1, chunks))] if chunks > 1 else [[0]]
    ka_cos, ka_sin, tables = column_tables(cols, devices, scale)

    arrived = []
    for classes in groups:
        x = head_stage(limbs_a, limbs_b, device.reshape(1), devices, classes, chunks)
        arrived.append(exchange(x))
    back = []
    for x, classes in zip(arrived, groups):
        q_cos, q_sin = spectral_turns(cols, devices, device, outer, classes, chunks, 4 * total)
        back.append(exchange(middle_stage(x, ka_cos, ka_sin, q_cos, q_sin, tables)))
    table = row_table(devices, device)
    parts = []
    for v, classes in zip(back, groups):
        rows = [row_turns(outer, devices, device, h, chunks) for h in classes]
        cos, sin = (jnp.concatenate(r, axis=0) for r in zip(*rows))
        parts.append(tail_stage(v, table, cos, sin, parts, classes, chunks, outer))
    return parts[-1]


def solution(mesh):
    placed = P(AXES, None)
    return jax.shard_map(
        on_device, mesh=mesh, in_specs=(placed, placed), out_specs=placed, check_vma=False
    )
```
